32 devices in a mesh: dp: 8 (over z, core), expert: 4 (over y, x).
Axes of the slice: x: 2, y: 2, z: 4, core: 2. Of those that a mesh axis runs over, the one named last changes fastest.
Arguments:
- tokens: bfloat16 [4, 1024, 2048], P('expert', 'dp'), may hold values from -6 to 6
- norm1: bfloat16 [2048], replicated, may hold values from 0.5 to 1.5
- w_query: bfloat16 [2048, 4096], P(('dp', 'expert')), may hold values from -0.125 to 0.125
- key_projection: bfloat16 [2048, 512], P(('dp', 'expert')), may hold values from -0.125 to 0.125
- value_projection: bfloat16 [2048, 512], P(('dp', 'expert')), may hold values from -0.125 to 0.125
- q_gain: bfloat16 [128], replicated, may hold values from 0.5 to 1.5
- key_norm_gain: bfloat16 [128], replicated, may hold values from 0.5 to 1.5
- w_out: bfloat16 [4096, 2048], P(('dp', 'expert')), may hold values from -0.5 to 0.5
- norm2: bfloat16 [2048], replicated, may hold values from 0.5 to 1.5
- w_router: bfloat16 [2048, 8], P(('dp', 'expert')), may hold values from -0.0625 to 0.0625
- w_gate: bfloat16 [8, 2048, 768], P('expert'), may hold values from -0.125 to 0.125
- w_up: bfloat16 [8, 2048, 768], P('expert'), may hold values from -0.125 to 0.125
- w_down: bfloat16 [8, 768, 2048], P('expert'), may hold values from -0.625 to 0.625
- segments: int32 [4, 1024], P('expert', 'dp'), may hold values from 0 to 7, never falling along the last dimension, each value on 1 to 512 neighbouring positions
- routes: int32 [4, 1024, 2], P('expert', 'dp'), may hold values from 0 to 7, all different within a row; in each aligned block of 128 rows (0 to 127, 128 to 255, ..., all dimensions but the last counted through in order) at most 48 rows name the same one
- grad_out: bfloat16 [4, 1024, 2048], P('expert', 'dp'), may hold values from -6 to 6
Outputs:
- output: bfloat16 [4, 1024, 2048], P('expert', 'dp')
- grad_input: float32 [4, 1024, 2048], P('expert', 'dp')
- grad_norm1: float32 [2048], replicated
- grad_w_query: float32 [2048, 4096], P(('dp', 'expert'))
- grad_w_key: float32 [2048, 512], P(('dp', 'expert'))
- grad_w_value: float32 [2048, 512], P(('dp', 'expert'))
- grad_q_gain: float32 [128], replicated
- grad_k_gain: float32 [128], replicated
- grad_w_out: float32 [4096, 2048], P(('dp', 'expert'))
- grad_norm2: float32 [2048], replicated
- grad_w_router: float32 [2048, 8], P(('dp', 'expert'))
- grad_w_gate: float32 [8, 2048, 768], P('expert', 'dp')
- grad_w_up: float32 [8, 2048, 768], P('expert', 'dp')
- grad_w_down: float32 [8, 768, 2048], P('expert', None, 'dp')
The draws below stay inside these ranges and needn't reach their ends.
Inputs may be any that keep to these rules, and one draw needn't show every extreme that they name: `segments`: along a sequence the document number never falls; each document has 1 to 512 tokens and some document has exactly 512. `routes`: A token names 2 different experts. Among the 128 tokens of one device no expert is named more than 48 times, and some expert reaches 48.
All inputs are finite; a program needn't handle non-finite values.
Results may differ from the reference program's by a relative error of at most 0.03.
Values may be sent and summed in bfloat16 or wider, within the bound.
No kernel may reach another device: no remote copies, remote signals or barrier semaphores. Data moves between devices by JAX's collectives and lax.ppermute only.
A program may use at most 256 MiB of HBM per device.

```python
import math
import jax
import jax.numpy as jnp
import numpy as np
from jax import lax

MODEL_WIDTH = 2048
QUERY_HEADS = 32
KV_HEAD_COUNT = 4
HEAD_SIZE = 128
FF = 768
NEXP = 8
TOP = 2
TOK_DEV = 128
CAP = 48
PACKED_TOKENS = 1024
GROUPS = 4


def block_levels(rng, dims, shards, least, largest):
    level = 1.0
    for dim, parts in shards:
        steps = jax.random.uniform(jax.random.fold_in(jax.random.fold_in(rng, 6), dim), (parts,), jnp.float32, least / len(shards), largest / len(shards))
        level = level * jnp.repeat(jnp.exp(steps), dims[dim] // parts).reshape((-1,) + (1,) * (len(dims) - 1 - dim))
    return level


def profile(amount, total, limit, skew):
    portions = [(1 << 20) // math.isqrt(rank ** skew) + 1 for rank in range(2, amount + 1)]
    rest, given = total - limit - (amount - 1), [1] * (amount - 1)
    while rest > 0:
        movable = [i for i in range(amount - 1) if given[i] < limit]
        pool, budget = sum([portions[i] for i in movable]), rest
        for i in movable:
            addition = min(limit - given[i], max(1, budget * portions[i] // pool), rest)
            given[i] = given[i] + addition
            rest = rest - addition
    return np.array([limit] + given)


def ragged_sizes(own_key, number_of, total, reach, slope):
    if number_of == 2:
        one = jax.random.randint(own_key, (), max(1, total - reach), min(reach, total - 1) + 1)
        return jnp.stack([one, total - one])
    tallies = jnp.asarray(profile(number_of, total, reach, slope), jnp.int32)
    couples = (number_of - 1) // 2
    donor, receiver = tallies[1:1 + 2 * couples:2], tallies[2:2 + 2 * couples:2]
    margin = jnp.minimum(donor - 1, reach - receiver)
    shifted = jax.random.randint(jax.random.fold_in(own_key, 1), (couples,), 0, 1 << 20) % (margin + 1)
    tallies = tallies.at[1:1 + 2 * couples:2].set(donor - shifted).at[2:2 + 2 * couples:2].set(receiver + shifted)
    return tallies[jax.random.permutation(jax.random.fold_in(own_key, 2), number_of)]


def deal_out(own_key, own, number, rows, number_of, top, bound, slope):
    order = jax.random.permutation(own_key, number_of)
    packed, ordinary = portions_of(number_of, rows * top, bound, slope, True), portions_of(number_of, rows * top, bound, slope, False)
    places = jnp.arange(number_of)

    def named(sizes, rotation):
        used = int((sizes > 0).sum())
        fixed = max(1, used // 4)
        shifted = fixed + (places - fixed + rotation * (used - fixed)) % max(1, number_of - fixed)
        return jnp.zeros((number_of,), jnp.int32).at[order[jnp.where(places < fixed, places, shifted)]].set(jnp.asarray(sizes, jnp.int32))

    sizes = jnp.where(number % 4 == 0, named(packed, number // 4), named(ordinary, number - number // 4 - 1))
    mixed = jax.random.permutation(jax.random.fold_in(own, 3), number_of)
    source_of, receiver = mixed[0:number_of // 2 * 2:2], mixed[1:number_of // 2 * 2:2]
    slack = jnp.minimum(sizes[source_of] - 1, bound - sizes[receiver]) // 2
    slack = jnp.where((source_of == order[0]) | (receiver == order[0]) | (sizes[receiver] == 0), 0, jnp.maximum(slack, 0))
    shifted = jax.random.randint(jax.random.fold_in(own, 4), (number_of // 2,), 0, 1 << 20) % (slack + 1)
    sizes = sizes.at[source_of].add(-shifted).at[receiver].add(shifted)
    members = jnp.searchsorted(jnp.cumsum(sizes), jnp.arange(rows * top), side="right").astype(jnp.int32)
    table = members.reshape(top, rows).T
    table = table[jax.random.permutation(jax.random.fold_in(own, 1), rows)]
    rotation = jax.random.randint(jax.random.fold_in(own, 2), (rows, 1), 0, top)
    return jnp.take_along_axis(table, (jnp.arange(top)[None, :] + rotation) % top, axis=1)


def portions_of(count, total, most, slope, full):
    portions = [(1 << 20) // math.isqrt(grade ** slope) + 1 for grade in range(1, count + 1)]
    largest = most if full else min(most, max(-(-total // count), total * portions[0] // sum(portions)))
    least = 1 if total - largest >= count - 1 else 0
    holding, spare = [largest] + [least] * (count - 1), total - largest - least * (count - 1)
    while spare > 0:
        movable = [i for i in range(1, count) if holding[i] < largest] or [i for i in range(1, count) if holding[i] < most]
        mass, left = sum([portions[i] for i in movable]), spare
        for i in movable:
            more = min(most - holding[i], max(1, left * portions[i] // mass), spare)
            holding[i] = holding[i] + more
            spare = spare - more
    return np.array(holding)


def normal_values(stream_key, extent, scale, bound, split=(), kind=jnp.bfloat16):
    values = scale * jax.random.normal(stream_key, extent, jnp.float32)
    if split:
        values = values * block_levels(stream_key, extent, split, -0.22, 0.18)
    return jnp.clip(values, -bound, bound).astype(kind)


def setup_inputs(seed: int = 0) -> dict:
    key_of = jax.random.split(jax.random.key(seed), 17)
    tokens = normal_values(key_of[0], (GROUPS, PACKED_TOKENS, MODEL_WIDTH), 1.0, 6.0, ((0, 4), (1, 8)))
    norm1 = jnp.clip(1.0 + 0.1 * jax.random.normal(key_of[1], (MODEL_WIDTH,), jnp.float32), 0.5, 1.5).astype(jnp.bfloat16)
    w_query = normal_values(key_of[2], (MODEL_WIDTH, QUERY_HEADS * HEAD_SIZE), MODEL_WIDTH ** -0.5, 0.125, ((0, 32),))
    key_projection = normal_values(key_of[3], (MODEL_WIDTH, KV_HEAD_COUNT * HEAD_SIZE), MODEL_WIDTH ** -0.5, 0.125, ((0, 32),))
    value_projection = normal_values(key_of[4], (MODEL_WIDTH, KV_HEAD_COUNT * HEAD_SIZE), MODEL_WIDTH ** -0.5, 0.125, ((0, 32),))
    q_gain = jnp.clip(1.0 + 0.1 * jax.random.normal(key_of[5], (HEAD_SIZE,), jnp.float32), 0.5, 1.5).astype(jnp.bfloat16)
    key_norm_gain = jnp.clip(1.0 + 0.1 * jax.random.normal(key_of[6], (HEAD_SIZE,), jnp.float32), 0.5, 1.5).astype(jnp.bfloat16)
    w_out = normal_values(key_of[7], (QUERY_HEADS * HEAD_SIZE, MODEL_WIDTH), (QUERY_HEADS * HEAD_SIZE // 32) ** -0.5, 0.5, ((0, 32),))
    norm2 = jnp.clip(1.0 + 0.1 * jax.random.normal(key_of[8], (MODEL_WIDTH,), jnp.float32), 0.5, 1.5).astype(jnp.bfloat16)
    w_router = normal_values(key_of[9], (MODEL_WIDTH, NEXP), (4 * MODEL_WIDTH) ** -0.5, 0.0625, ((0, 32),))
    w_gate = normal_values(key_of[10], (NEXP, MODEL_WIDTH, FF), MODEL_WIDTH ** -0.5, 0.125, ((0, 4),))
    w_up = normal_values(key_of[11], (NEXP, MODEL_WIDTH, FF), MODEL_WIDTH ** -0.5, 0.125, ((0, 4),))
    w_down = normal_values(key_of[12], (NEXP, FF, MODEL_WIDTH), (FF // 8) ** -0.5, 0.625, ((0, 4),))
    segments = jax.vmap(lambda own: jnp.searchsorted(jnp.cumsum(ragged_sizes(own, 8, PACKED_TOKENS, PACKED_TOKENS // 2, 2)), jnp.arange(PACKED_TOKENS), side="right"))(jax.random.split(key_of[13], GROUPS)).reshape((GROUPS, PACKED_TOKENS)).astype(jnp.int32)
    routes_keys = jax.random.split(jax.random.fold_in(key_of[14], 1), GROUPS * PACKED_TOKENS // TOK_DEV)
    routes_turns = jax.random.permutation(jax.random.fold_in(key_of[14], 3), GROUPS * PACKED_TOKENS // TOK_DEV)
    routes = jax.vmap(lambda own, number: deal_out(jax.random.fold_in(key_of[14], 2), own, number, TOK_DEV, NEXP, TOP, CAP, 1))(routes_keys, routes_turns).reshape((GROUPS, PACKED_TOKENS, TOP))
    grad_out = normal_values(key_of[15], (GROUPS, PACKED_TOKENS, MODEL_WIDTH), 1.0, 6.0, ((0, 4), (1, 8)))
    return dict(tokens=tokens, norm1=norm1, w_query=w_query, key_projection=key_projection, value_projection=value_projection, q_gain=q_gain, key_norm_gain=key_norm_gain, w_out=w_out, norm2=norm2, w_router=w_router, w_gate=w_gate, w_up=w_up, w_down=w_down, segments=segments, routes=routes, grad_out=grad_out)


EPSILON = 1e-06
THETA_BASE = 1000000.0
MASKED = -1e+30

@jax.custom_vjp
def reduced_precision(v):
    return lax.optimization_barrier(v.astype(jnp.bfloat16)).astype(jnp.float32)

@jax.custom_vjp
def reduced_backward(v):
    return v

def low_keep(v):
    return (reduced_precision(v), None)

def low_pass(kept, grad):
    return (grad,)

def back_keep(v):
    return (v, None)

def back_low(kept, grad):
    return (reduced_precision(grad),)
reduced_precision.defvjp(low_keep, low_pass)
reduced_backward.defvjp(back_keep, back_low)

def matrix_product(left, right):
    return jnp.dot(left, right, precision=lax.Precision.HIGHEST, preferred_element_type=jnp.float32)

def norm_rows(values, gain):
    return values * lax.rsqrt(lax.optimization_barrier(jnp.mean(values * values, axis=-1, keepdims=True)) + EPSILON) * gain

def rotate_half(values):
    middle = values.shape[-1] // 2
    return jnp.concatenate([-values[..., middle:], values[..., :middle]], axis=-1)

def rope_tables(positions, head_width):
    freq_index = jnp.arange(head_width // 2).astype(jnp.float32)
    inverse = THETA_BASE ** (-2.0 * freq_index / head_width)
    angles = positions.astype(jnp.float32)[:, None] * inverse[None, :]
    angles = jnp.concatenate([angles, angles], axis=-1)
    return (jnp.cos(angles)[:, None, :], jnp.sin(angles)[:, None, :])

def prepare_heads(raw, gain, cosine_table, sine_table, heads):
    normed = norm_rows(raw.reshape(raw.shape[0], heads, -1), gain)
    return normed * cosine_table + rotate_half(normed) * sine_table

def attend(query_rows, keys_all, values_all, segment):
    block_length = min(512, PACKED_TOKENS)
    block_total = PACKED_TOKENS // block_length
    group_width = QUERY_HEADS // KV_HEAD_COUNT
    score_scale = HEAD_SIZE ** (-0.5)
    query_block_list = query_rows.reshape(block_total, block_length, KV_HEAD_COUNT, group_width, HEAD_SIZE)
    block_starts = jnp.arange(block_total, dtype=jnp.int32) * block_length
    key_pos = jnp.arange(PACKED_TOKENS, dtype=jnp.int32)

    def one_block(block_item):
        query_blk, start_row = block_item
        query_pos = start_row + jnp.arange(block_length, dtype=jnp.int32)
        query_seg = lax.dynamic_slice_in_dim(segment, start_row, block_length)
        score = jnp.einsum('tkgd,skd->kgts', query_blk, keys_all, precision=lax.Precision.HIGHEST) * score_scale
        score = reduced_backward(score)
        allowed = (query_pos[:, None] >= key_pos[None, :]) & (query_seg[:, None] == segment[None, :])
        score = jnp.where(allowed[None, None], score, MASKED)
        weights = reduced_precision(jax.nn.softmax(score, axis=-1))
        mixed_out = jnp.einsum('kgts,skd->tkgd', weights, values_all, precision=lax.Precision.HIGHEST)
        return mixed_out.reshape(block_length, QUERY_HEADS * HEAD_SIZE)
    return lax.map(jax.checkpoint(one_block), (query_block_list, block_starts)).reshape(PACKED_TOKENS, QUERY_HEADS * HEAD_SIZE)

def layer(params, seq_tokens, segment, chosen):
    norm1, w_query, key_projection, value_projection, q_gain, key_norm_gain, w_out, norm2, w_router, w_gate, w_up, w_down = params
    first_normed = reduced_precision(norm_rows(seq_tokens, norm1))
    q_raw = reduced_backward(matrix_product(first_normed, w_query))
    key_unrotated = reduced_backward(matrix_product(first_normed, key_projection))
    value_reduced = reduced_precision(reduced_backward(matrix_product(first_normed, value_projection))).reshape(PACKED_TOKENS, KV_HEAD_COUNT, HEAD_SIZE)
    cosine_table, sine_table = rope_tables(jnp.arange(PACKED_TOKENS, dtype=jnp.int32), HEAD_SIZE)
    q_low = reduced_precision(prepare_heads(q_raw, q_gain, cosine_table, sine_table, QUERY_HEADS))
    key_reduced = reduced_precision(prepare_heads(key_unrotated, key_norm_gain, cosine_table, sine_table, KV_HEAD_COUNT))
    attn_low = reduced_precision(reduced_backward(attend(q_low, key_reduced, value_reduced, segment)))
    residual = seq_tokens + reduced_backward(matrix_product(attn_low, w_out))
    normed2 = reduced_precision(norm_rows(residual, norm2))
    logits = reduced_backward(matrix_product(normed2, w_router))
    picked = jnp.take_along_axis(logits, chosen, axis=1)
    gate_probs = jax.nn.softmax(picked, axis=-1)
    onehot = (chosen[:, :, None] == jnp.arange(NEXP, dtype=jnp.int32)[None, None, :]).astype(jnp.float32)
    combine = lax.optimization_barrier(jnp.sum(onehot * gate_probs[:, :, None], axis=1))

    def expert_step(running, expert_item):
        gate_w, up_w, down_w, weight_col = expert_item
        expert_in = reduced_backward(normed2)
        gate_pre = reduced_backward(matrix_product(expert_in, gate_w))
        up_pre = reduced_backward(matrix_product(expert_in, up_w))
        hidden = reduced_precision(jax.nn.silu(gate_pre) * up_pre)
        expert_out = reduced_precision(reduced_backward(matrix_product(hidden, down_w)))
        return (running + weight_col[:, None] * expert_out, None)
    mixture, _ = lax.scan(jax.checkpoint(expert_step), jnp.zeros((PACKED_TOKENS, MODEL_WIDTH), jnp.float32), (w_gate, w_up, w_down, combine.T))
    return residual + mixture

def reference(tokens, norm1, w_query, key_projection, value_projection, q_gain, key_norm_gain, w_out, norm2, w_router, w_gate, w_up, w_down, segments, routes, grad_out):
    params = tuple((weight.astype(jnp.float32) for weight in (norm1, w_query, key_projection, value_projection, q_gain, key_norm_gain, w_out, norm2, w_router, w_gate, w_up, w_down)))

    def per_sequence(summed, seq_item):
        seq_tokens, seq_segments, seq_routes, seq_grad = seq_item
        result, pull_back = jax.vjp(lambda weights, inputs: layer(weights, inputs, seq_segments, seq_routes), params, seq_tokens.astype(jnp.float32))
        weight_grads, input_grad = pull_back(seq_grad.astype(jnp.float32))
        summed = jax.tree.map(lambda left, right: left + right, summed, weight_grads)
        return (summed, (result.astype(jnp.bfloat16), input_grad))
    zero_grads = jax.tree.map(jnp.zeros_like, params)
    totals, (outputs, input_grads) = lax.scan(per_sequence, zero_grads, (tokens, segments, routes, grad_out))
    return (outputs, input_grads, totals[0], totals[1], totals[2], totals[3], totals[4], totals[5], totals[6], totals[7], totals[8], totals[9], totals[10], totals[11])
```

```python
import jax
import jax.numpy as jnp
from jax import lax
from jax.sharding import PartitionSpec as P

CAP = 48


EPSILON = 1e-06
THETA_BASE = 1000000.0
MASKED = -1e30


def norm_rows(values, gain):
    return values * lax.rsqrt(jnp.mean(values * values, axis=-1, keepdims=True) + EPSILON) * gain


def rotate_half(values):
    middle = values.shape[-1] // 2
    return jnp.concatenate([-values[..., middle:], values[..., :middle]], axis=-1)


def rope_tables(positions, head_width):
    freq_index = jnp.arange(head_width // 2).astype(jnp.float32)
    inverse = THETA_BASE ** (-2.0 * freq_index / head_width)
    angles = positions.astype(jnp.float32)[:, None] * inverse[None, :]
    angles = jnp.concatenate([angles, angles], axis=-1)
    return (jnp.cos(angles)[:, None, :], jnp.sin(angles)[:, None, :])


def prepare_heads(raw, gain, cosine_table, sine_table, heads):
    normed = norm_rows(raw.reshape(raw.shape[0], heads, -1), gain)
    return normed * cosine_table + rotate_half(normed) * sine_table


def silu_product(gate_pre, up_pre):
    return jax.nn.silu(gate_pre) * up_pre


def shards(
    tokens,
    norm1,
    w_query,
    key_projection,
    value_projection,
    q_gain,
    key_norm_gain,
    w_out,
    norm2,
    w_router,
    w_gate,
    w_up,
    w_down,
    segments,
    routes,
    grad_out,
):
    tok_in = tokens[0].astype(jnp.float32)
    tok_rows, model_dim = tok_in.shape
    head_dim = q_gain.shape[0]
    heads_q = w_query.shape[1] // head_dim
    heads_kv = key_projection.shape[1] // head_dim
    n_dp = lax.axis_size("dp")
    n_expert = lax.axis_size("expert")
    w_rows = w_query.shape[0]
    own_heads = heads_q // n_dp
    share = n_dp // heads_kv
    q_cols = own_heads * head_dim
    n_routed = w_router.shape[1]
    top_count = routes.shape[2]
    score_scale = head_dim ** (-0.5)
    gain_one = norm1.astype(jnp.float32)
    gain_two = norm2.astype(jnp.float32)
    gain_query = q_gain.astype(jnp.float32)
    gain_key = key_norm_gain.astype(jnp.float32)
    normed1_f, norm1_pull = jax.vjp(norm_rows, tok_in, gain_one)
    first_normed = lax.all_gather(normed1_f.astype(jnp.bfloat16), "dp", axis=0, tiled=True)
    segment = lax.all_gather(segments[0].astype(jnp.bfloat16), "dp", axis=0, tiled=True)
    seq_rows = first_normed.shape[0]

    def spread_heads(matrix):
        return jnp.repeat(matrix.reshape(w_rows, heads_kv, head_dim), share, axis=1)

    router_pad = jnp.pad(w_router, ((0, 0), (0, head_dim - n_routed)))
    blocks = jnp.concatenate(
        [
            w_query.reshape(w_rows, n_dp, q_cols),
            spread_heads(key_projection),
            spread_heads(value_projection),
            jnp.broadcast_to(router_pad[:, None, :], (w_rows, n_dp, head_dim)),
        ],
        axis=2,
    ).transpose(1, 0, 2)
    blocks = lax.all_to_all(blocks, "dp", split_axis=0, concat_axis=0, tiled=True)
    blocks = lax.all_gather(blocks, "expert", axis=0)
    own_weights = blocks.transpose(1, 0, 2, 3).reshape(model_dim, -1)
    qkv_cols = q_cols + 2 * head_dim
    full_router = own_weights[:, qkv_cols : qkv_cols + n_routed]
    own_weights = own_weights[:, :qkv_cols]
    own_out = lax.all_gather(w_out, "expert", axis=0, tiled=True)
    raw = jnp.dot(first_normed, own_weights, preferred_element_type=jnp.float32)
    q_raw = raw[:, :q_cols]
    key_unrotated = raw[:, q_cols : q_cols + head_dim]
    value_low = raw[:, q_cols + head_dim :].astype(jnp.bfloat16)
    positions = jnp.arange(seq_rows, dtype=jnp.int32)
    cosine_table, sine_table = rope_tables(positions, head_dim)
    q_rot, query_pull = jax.vjp(
        lambda raw_in, gain_in: prepare_heads(raw_in, gain_in, cosine_table, sine_table, own_heads),
        q_raw,
        gain_query,
    )
    k_rot, key_pull = jax.vjp(
        lambda raw_in, gain_in: prepare_heads(raw_in, gain_in, cosine_table, sine_table, 1),
        key_unrotated,
        gain_key,
    )
    q_low = q_rot.astype(jnp.bfloat16)
    key_low = k_rot.astype(jnp.bfloat16).reshape(seq_rows, head_dim)
    allowed = (
        (positions[:, None] >= positions[None, :]) & (segment[:, None] == segment[None, :])
    )[None]

    def raw_weights():
        score = jnp.einsum("tgd,sd->gts", q_low, key_low, preferred_element_type=jnp.float32)
        return jnp.where(allowed, jnp.exp(score * score_scale), 0.0)

    weights = raw_weights()
    inverse_sum = 1.0 / jnp.sum(weights, axis=-1)
    attn_heads = (
        jnp.einsum(
            "gts,sd->gtd", weights.astype(jnp.bfloat16), value_low, preferred_element_type=jnp.float32
        )
        * inverse_sum[..., None]
    )
    attn_low = attn_heads.transpose(1, 0, 2).reshape(seq_rows, q_cols).astype(jnp.bfloat16)
    branch_term = jnp.dot(attn_low, own_out, preferred_element_type=jnp.float32)
    branch = lax.psum_scatter(
        branch_term.astype(jnp.bfloat16), "dp", scatter_dimension=0, tiled=True
    )
    residual = tok_in + branch.astype(jnp.float32)
    normed2_f, norm2_pull = jax.vjp(norm_rows, residual, gain_two)
    normed2 = normed2_f.astype(jnp.bfloat16)
    logits = jnp.dot(normed2, full_router, preferred_element_type=jnp.float32)
    chosen = routes[0]
    gate_probs, gate_pull = jax.vjp(
        lambda logit_in: jax.nn.softmax(jnp.take_along_axis(logit_in, chosen, axis=1), axis=-1),
        logits,
    )
    flat_routes = chosen.reshape(-1)
    onehot = (flat_routes[:, None] == jnp.arange(n_routed, dtype=jnp.int32)[None, :]).astype(
        jnp.int32
    )
    ranks = jnp.sum((jnp.cumsum(onehot, axis=0) - 1) * onehot, axis=1)
    slots = flat_routes * CAP + ranks
    token_of = jnp.arange(tok_rows * top_count, dtype=jnp.int32) // top_count
    send_rows = (
        jnp.zeros((n_routed * CAP, model_dim), jnp.bfloat16)
        .at[slots]
        .set(normed2[token_of])
        .reshape(n_routed, CAP, model_dim)
    )
    received = lax.all_to_all(send_rows, "expert", split_axis=0, concat_axis=1, tiled=True)
    gate_pre = jnp.einsum("erd,edf->erf", received, w_gate, preferred_element_type=jnp.float32)
    up_pre = jnp.einsum("erd,edf->erf", received, w_up, preferred_element_type=jnp.float32)
    hidden_f, act_pull = jax.vjp(silu_product, gate_pre, up_pre)
    hidden = hidden_f.astype(jnp.bfloat16)
    expert_out = jnp.einsum(
        "erf,efd->erd", hidden, w_down, preferred_element_type=jnp.float32
    ).astype(jnp.bfloat16)
    returned = lax.all_to_all(
        expert_out, "expert", split_axis=1, concat_axis=0, tiled=True
    ).reshape(n_routed * CAP, model_dim)
    route_out = returned[slots].astype(jnp.float32).reshape(tok_rows, top_count, model_dim)
    mixture = jnp.sum(gate_probs[:, :, None] * route_out, axis=1)
    output = (residual + mixture).astype(jnp.bfloat16)[None]
    grad_rows = grad_out[0].astype(jnp.float32)
    d_gates = jnp.sum(grad_rows[:, None, :] * route_out, axis=-1)
    d_logits = gate_pull(d_gates)[0].astype(jnp.bfloat16)
    d_route = (
        (gate_probs[:, :, None] * grad_rows[:, None, :])
        .astype(jnp.bfloat16)
        .reshape(tok_rows * top_count, model_dim)
    )
    d_send = (
        jnp.zeros((n_routed * CAP, model_dim), jnp.bfloat16)
        .at[slots]
        .set(d_route)
        .reshape(n_routed, CAP, model_dim)
    )
    d_recv = lax.all_to_all(d_send, "expert", split_axis=0, concat_axis=1, tiled=True)
    d_hidden = jnp.einsum("erd,efd->erf", d_recv, w_down, preferred_element_type=jnp.float32)
    grad_down = jnp.einsum("erf,erd->efd", hidden, d_recv, preferred_element_type=jnp.float32)
    d_gate_f, d_up_f = act_pull(d_hidden)
    d_gate = d_gate_f.astype(jnp.bfloat16)
    d_up = d_up_f.astype(jnp.bfloat16)
    grad_gate = jnp.einsum("erd,erf->edf", received, d_gate, preferred_element_type=jnp.float32)
    grad_upper = jnp.einsum("erd,erf->edf", received, d_up, preferred_element_type=jnp.float32)
    d_in = (
        jnp.einsum("erf,edf->erd", d_gate, w_gate, preferred_element_type=jnp.float32)
        + jnp.einsum("erf,edf->erd", d_up, w_up, preferred_element_type=jnp.float32)
    ).astype(jnp.bfloat16)
    d_back = lax.all_to_all(d_in, "expert", split_axis=1, concat_axis=0, tiled=True).reshape(
        n_routed * CAP, model_dim
    )
    d_normed2 = jnp.sum(
        d_back[slots].astype(jnp.float32).reshape(tok_rows, top_count, model_dim), axis=1
    )
    d_normed2 = d_normed2 + jnp.einsum(
        "te,de->td", d_logits, full_router, preferred_element_type=jnp.float32
    )
    d_resid_norm, grad_gain_two = norm2_pull(d_normed2)
    d_resid = grad_rows + d_resid_norm
    d_branch = d_resid.astype(jnp.bfloat16)
    all_branch = lax.all_gather(d_branch, "dp", axis=0, tiled=True)
    d_attn = jnp.einsum(
        "td,cd->tc", all_branch, own_out, preferred_element_type=jnp.float32
    ).astype(jnp.bfloat16)
    d_attn_heads = d_attn.reshape(seq_rows, own_heads, head_dim)
    delta = jnp.sum(d_attn_heads.transpose(1, 0, 2).astype(jnp.float32) * attn_heads, axis=-1)
    probs = raw_weights() * inverse_sum[..., None]
    d_probs = jnp.einsum(
        "tgd,sd->gts", d_attn_heads, value_low, preferred_element_type=jnp.float32
    )
    d_score = (probs * (d_probs - delta[..., None])).astype(jnp.bfloat16)
    d_query = score_scale * jnp.einsum(
        "gts,sd->tgd", d_score, key_low, preferred_element_type=jnp.float32
    )
    d_keys = score_scale * jnp.einsum(
        "gts,tgd->sd", d_score, q_low, preferred_element_type=jnp.float32
    )
    d_values = jnp.einsum(
        "gts,tgd->sd", probs.astype(jnp.bfloat16), d_attn_heads, preferred_element_type=jnp.float32
    )
    d_q_f, grad_gain_query = query_pull(d_query)
    d_k_f, grad_gain_key = key_pull(d_keys[:, None, :])
    d_qkv = jnp.concatenate([d_q_f, d_k_f, d_values], axis=1).astype(jnp.bfloat16)
    normed1_term = jnp.einsum("tc,dc->td", d_qkv, own_weights, preferred_element_type=jnp.float32)
    d_normed1 = lax.psum_scatter(
        normed1_term.astype(jnp.bfloat16), "dp", scatter_dimension=0, tiled=True
    ).astype(jnp.float32)
    d_tok_norm, grad_gain_one = norm1_pull(d_normed1)
    grad_input = (d_resid + d_tok_norm)[None]
    sum_one, sum_query, sum_key, sum_two = lax.psum(
        (grad_gain_one, grad_gain_query, grad_gain_key, grad_gain_two), ("dp", "expert")
    )
    sum_gate, sum_upper, sum_down = (
        lax.psum_scatter(
            grad_gate.astype(jnp.bfloat16), "dp", scatter_dimension=1, tiled=True
        ).astype(jnp.float32),
        lax.psum_scatter(
            grad_upper.astype(jnp.bfloat16), "dp", scatter_dimension=1, tiled=True
        ).astype(jnp.float32),
        lax.psum_scatter(
            grad_down.astype(jnp.bfloat16), "dp", scatter_dimension=2, tiled=True
        ).astype(jnp.float32),
    )
    qkv_term = jnp.einsum("td,tc->dc", first_normed, d_qkv, preferred_element_type=jnp.float32)
    router_term = jnp.einsum("td,te->de", normed2, d_logits, preferred_element_type=jnp.float32)
    router_term = jnp.pad(router_term, ((0, 0), (0, head_dim - n_routed)))
    grad_blocks = (
        jnp.concatenate([qkv_term, router_term], axis=1)
        .astype(jnp.bfloat16)
        .reshape(n_dp, n_expert, w_rows, -1)
        .transpose(1, 0, 2, 3)
        .reshape(model_dim, -1)
    )
    grad_blocks = lax.psum_scatter(grad_blocks, "expert", scatter_dimension=0, tiled=True)
    grad_blocks = grad_blocks.reshape(n_dp, w_rows, -1)
    grad_blocks = lax.all_to_all(
        grad_blocks, "dp", split_axis=0, concat_axis=0, tiled=True
    ).astype(jnp.float32)

    def gather_heads(first):
        picked = grad_blocks[:, :, first : first + head_dim]
        picked = jnp.sum(picked.reshape(heads_kv, share, w_rows, head_dim), axis=1)
        return picked.transpose(1, 0, 2).reshape(w_rows, heads_kv * head_dim)

    sum_wq = grad_blocks[:, :, :q_cols].transpose(1, 0, 2).reshape(w_rows, heads_q * head_dim)
    sum_wk = gather_heads(q_cols)
    sum_wv = gather_heads(q_cols + head_dim)
    sum_wr = jnp.sum(grad_blocks[:, :, qkv_cols : qkv_cols + n_routed], axis=0)
    out_term = jnp.einsum("tc,td->cd", attn_low, all_branch, preferred_element_type=jnp.float32)
    sum_wo = lax.psum_scatter(
        out_term.astype(jnp.bfloat16), "expert", scatter_dimension=0, tiled=True
    ).astype(jnp.float32)
    return (
        output,
        grad_input,
        sum_one,
        sum_wq,
        sum_wk,
        sum_wv,
        sum_query,
        sum_key,
        sum_wo,
        sum_two,
        sum_wr,
        sum_gate,
        sum_upper,
        sum_down,
    )


def solution(mesh):
    return jax.shard_map(
        shards,
        mesh=mesh,
        in_specs=(
            P("expert", "dp", None),
            P(),
            P(("dp", "expert"), None),
            P(("dp", "expert"), None),
            P(("dp", "expert"), None),
            P(),
            P(),
            P(("dp", "expert"), None),
            P(),
            P(("dp", "expert"), None),
            P("expert", None, None),
            P("expert", None, None),
            P("expert", None, None),
            P("expert", "dp"),
            P("expert", "dp", None),
            P("expert", "dp", None),
        ),
        out_specs=(
            P("expert", "dp", None),
            P("expert", "dp", None),
            P(),
            P(("dp", "expert"), None),
            P(("dp", "expert"), None),
            P(("dp", "expert"), None),
            P(),
            P(),
            P(("dp", "expert"), None),
            P(),
            P(("dp", "expert"), None),
            P("expert", "dp", None),
            P("expert", "dp", None),
            P("expert", None, "dp"),
        ),
        check_vma=False,
    )
```

```python
import jax
import jax.numpy as jnp
from jax import lax
from jax.sharding import PartitionSpec as P

CAP = 48


EPSILON = 1e-06
THETA_BASE = 1000000.0
MASKED = -1e30


def norm_rows(values, gain):
    return values * lax.rsqrt(jnp.mean(values * values, axis=-1, keepdims=True) + EPSILON) * gain


def rotate_half(values):
    middle = values.shape[-1] // 2
    return jnp.concatenate([-values[..., middle:], values[..., :middle]], axis=-1)


def rope_tables(positions, head_width):
    freq_index = jnp.arange(head_width // 2).astype(jnp.float32)
    inverse = THETA_BASE ** (-2.0 * freq_index / head_width)
    angles = positions.astype(jnp.float32)[:, None] * inverse[None, :]
    angles = jnp.concatenate([angles, angles], axis=-1)
    return (jnp.cos(angles)[:, None, :], jnp.sin(angles)[:, None, :])


def prepare_heads(raw, gain, cosine_table, sine_table, heads):
    normed = norm_rows(raw.reshape(raw.shape[0], heads, -1), gain)
    return normed * cosine_table + rotate_half(normed) * sine_table


def silu_product(gate_pre, up_pre):
    return jax.nn.silu(gate_pre) * up_pre


def shards(
    tokens,
    norm1,
    w_query,
    key_projection,
    value_projection,
    q_gain,
    key_norm_gain,
    w_out,
    norm2,
    w_router,
    w_gate,
    w_up,
    w_down,
    segments,
    routes,
    grad_out,
):
    tok_in = tokens[0].astype(jnp.float32)
    tok_rows, model_dim = tok_in.shape
    head_dim = q_gain.shape[0]
    heads_q = w_query.shape[1] // head_dim
    heads_kv = key_projection.shape[1] // head_dim
    n_dp = lax.axis_size("dp")
    n_expert = lax.axis_size("expert")
    w_rows = w_query.shape[0]
    own_heads = heads_q // n_dp
    share = n_dp // heads_kv
    q_cols = own_heads * head_dim
    n_routed = w_router.shape[1]
    top_count = routes.shape[2]
    score_scale = head_dim ** (-0.5)
    gain_one = norm1.astype(jnp.float32)
    gain_two = norm2.astype(jnp.float32)
    gain_query = q_gain.astype(jnp.float32)
    gain_key = key_norm_gain.astype(jnp.float32)
    normed1_f, norm1_pull = jax.vjp(norm_rows, tok_in, gain_one)
    first_normed = lax.all_gather(normed1_f.astype(jnp.bfloat16), "dp", axis=0, tiled=True)
    segment = lax.all_gather(segments[0].astype(jnp.bfloat16), "dp", axis=0, tiled=True)
    seq_rows = first_normed.shape[0]

    def spread_heads(matrix):
        return jnp.repeat(matrix.reshape(w_rows, heads_kv, head_dim), share, axis=1)

    router_pad = jnp.pad(w_router, ((0, 0), (0, head_dim - n_routed)))
    blocks = jnp.concatenate(
        [
            w_query.reshape(w_rows, n_dp, q_cols),
            spread_heads(key_projection),
            spread_heads(value_projection),
            jnp.broadcast_to(router_pad[:, None, :], (w_rows, n_dp, head_dim)),
        ],
        axis=2,
    ).transpose(1, 0, 2)
    blocks = lax.all_to_all(blocks, "dp", split_axis=0, concat_axis=0, tiled=True)
    blocks = lax.all_to_all(
        jnp.broadcast_to(blocks[None], (n_expert,) + blocks.shape),
        "expert",
        split_axis=0,
        concat_axis=0,
        tiled=True,
    )
    own_weights = blocks.transpose(1, 0, 2, 3).reshape(model_dim, -1)
    qkv_cols = q_cols + 2 * head_dim
    full_router = own_weights[:, qkv_cols : qkv_cols + n_routed]
    own_weights = own_weights[:, :qkv_cols]
    own_out = lax.all_gather(w_out, "expert", axis=0, tiled=True)
    raw = jnp.dot(first_normed, own_weights, preferred_element_type=jnp.float32)
    q_raw = raw[:, :q_cols]
    key_unrotated = raw[:, q_cols : q_cols + head_dim]
    value_low = raw[:, q_cols + head_dim :].astype(jnp.bfloat16)
    positions = jnp.arange(seq_rows, dtype=jnp.int32)
    cosine_table, sine_table = rope_tables(positions, head_dim)
    q_rot, query_pull = jax.vjp(
        lambda raw_in, gain_in: prepare_heads(raw_in, gain_in, cosine_table, sine_table, own_heads),
        q_raw,
        gain_query,
    )
    k_rot, key_pull = jax.vjp(
        lambda raw_in, gain_in: prepare_heads(raw_in, gain_in, cosine_table, sine_table, 1),
        key_unrotated,
        gain_key,
    )
    q_low = q_rot.astype(jnp.bfloat16)
    key_low = k_rot.astype(jnp.bfloat16).reshape(seq_rows, head_dim)
    allowed = (
        (positions[:, None] >= positions[None, :]) & (segment[:, None] == segment[None, :])
    )[None]

    def raw_weights():
        score = jnp.einsum("tgd,sd->gts", q_low, key_low, preferred_element_type=jnp.float32)
        return jnp.where(allowed, jnp.exp(score * score_scale), 0.0)

    weights = raw_weights()
    inverse_sum = 1.0 / jnp.sum(weights, axis=-1)
    attn_heads = (
        jnp.einsum(
            "gts,sd->gtd", weights.astype(jnp.bfloat16), value_low, preferred_element_type=jnp.float32
        )
        * inverse_sum[..., None]
    )
    attn_low = attn_heads.transpose(1, 0, 2).reshape(seq_rows, q_cols).astype(jnp.bfloat16)
    branch_term = jnp.dot(attn_low, own_out, preferred_element_type=jnp.float32)
    branch = lax.psum_scatter(
        branch_term.astype(jnp.bfloat16), "dp", scatter_dimension=0, tiled=True
    )
    residual = tok_in + branch.astype(jnp.float32)
    normed2_f, norm2_pull = jax.vjp(norm_rows, residual, gain_two)
    normed2 = normed2_f.astype(jnp.bfloat16)
    logits = jnp.dot(normed2, full_router, preferred_element_type=jnp.float32)
    chosen = routes[0]
    gate_probs, gate_pull = jax.vjp(
        lambda logit_in: jax.nn.softmax(jnp.take_along_axis(logit_in, chosen, axis=1), axis=-1),
        logits,
    )
    flat_routes = chosen.reshape(-1)
    onehot = (flat_routes[:, None] == jnp.arange(n_routed, dtype=jnp.int32)[None, :]).astype(
        jnp.int32
    )
    ranks = jnp.sum((jnp.cumsum(onehot, axis=0) - 1) * onehot, axis=1)
    slots = flat_routes * CAP + ranks
    token_of = jnp.arange(tok_rows * top_count, dtype=jnp.int32) // top_count
    send_rows = (
        jnp.zeros((n_routed * CAP, model_dim), jnp.bfloat16)
        .at[slots]
        .set(normed2[token_of])
        .reshape(n_routed, CAP, model_dim)
    )
    received = lax.all_to_all(send_rows, "expert", split_axis=0, concat_axis=1, tiled=True)
    gate_pre = jnp.einsum("erd,edf->erf", received, w_gate, preferred_element_type=jnp.float32)
    up_pre = jnp.einsum("erd,edf->erf", received, w_up, preferred_element_type=jnp.float32)
    hidden_f, act_pull = jax.vjp(silu_product, gate_pre, up_pre)
    hidden = hidden_f.astype(jnp.bfloat16)
    expert_out = jnp.einsum(
        "erf,efd->erd", hidden, w_down, preferred_element_type=jnp.float32
    ).astype(jnp.bfloat16)
    returned = lax.all_to_all(
        expert_out, "expert", split_axis=1, concat_axis=0, tiled=True
    ).reshape(n_routed * CAP, model_dim)
    route_out = returned[slots].astype(jnp.float32).reshape(tok_rows, top_count, model_dim)
    mixture = jnp.sum(gate_probs[:, :, None] * route_out, axis=1)
    output = (residual + mixture).astype(jnp.bfloat16)[None]
    grad_rows = grad_out[0].astype(jnp.float32)
    d_gates = jnp.sum(grad_rows[:, None, :] * route_out, axis=-1)
    d_logits = gate_pull(d_gates)[0].astype(jnp.bfloat16)
    d_route = (
        (gate_probs[:, :, None] * grad_rows[:, None, :])
        .astype(jnp.bfloat16)
        .reshape(tok_rows * top_count, model_dim)
    )
    d_send = (
        jnp.zeros((n_routed * CAP, model_dim), jnp.bfloat16)
        .at[slots]
        .set(d_route)
        .reshape(n_routed, CAP, model_dim)
    )
    d_recv = lax.all_to_all(d_send, "expert", split_axis=0, concat_axis=1, tiled=True)
    d_hidden = jnp.einsum("erd,efd->erf", d_recv, w_down, preferred_element_type=jnp.float32)
    grad_down = jnp.einsum("erf,erd->efd", hidden, d_recv, preferred_element_type=jnp.float32)
    d_gate_f, d_up_f = act_pull(d_hidden)
    d_gate = d_gate_f.astype(jnp.bfloat16)
    d_up = d_up_f.astype(jnp.bfloat16)
    grad_gate = jnp.einsum("erd,erf->edf", received, d_gate, preferred_element_type=jnp.float32)
    grad_upper = jnp.einsum("erd,erf->edf", received, d_up, preferred_element_type=jnp.float32)
    d_in = (
        jnp.einsum("erf,edf->erd", d_gate, w_gate, preferred_element_type=jnp.float32)
        + jnp.einsum("erf,edf->erd", d_up, w_up, preferred_element_type=jnp.float32)
    ).astype(jnp.bfloat16)
    d_back = lax.all_to_all(d_in, "expert", split_axis=1, concat_axis=0, tiled=True).reshape(
        n_routed * CAP, model_dim
    )
    d_normed2 = jnp.sum(
        d_back[slots].astype(jnp.float32).reshape(tok_rows, top_count, model_dim), axis=1
    )
    d_normed2 = d_normed2 + jnp.einsum(
        "te,de->td", d_logits, full_router, preferred_element_type=jnp.float32
    )
    d_resid_norm, grad_gain_two = norm2_pull(d_normed2)
    d_resid = grad_rows + d_resid_norm
    sum_down = lax.psum_scatter(
        grad_down.astype(jnp.bfloat16), "dp", scatter_dimension=2, tiled=True
    )
    d_branch, sum_down = lax.optimization_barrier((d_resid.astype(jnp.bfloat16), sum_down))
    all_branch = lax.all_gather(d_branch, "dp", axis=0, tiled=True)
    gate_low, all_branch = lax.optimization_barrier((grad_gate.astype(jnp.bfloat16), all_branch))
    sum_gate = lax.psum_scatter(gate_low, "dp", scatter_dimension=1, tiled=True)
    d_attn = jnp.einsum(
        "td,cd->tc", all_branch, own_out, preferred_element_type=jnp.float32
    ).astype(jnp.bfloat16)
    d_attn_heads = d_attn.reshape(seq_rows, own_heads, head_dim)
    delta = jnp.sum(d_attn_heads.transpose(1, 0, 2).astype(jnp.float32) * attn_heads, axis=-1)
    probs = raw_weights() * inverse_sum[..., None]
    d_probs = jnp.einsum(
        "tgd,sd->gts", d_attn_heads, value_low, preferred_element_type=jnp.float32
    )
    d_score = (probs * (d_probs - delta[..., None])).astype(jnp.bfloat16)
    d_query = score_scale * jnp.einsum(
        "gts,sd->tgd", d_score, key_low, preferred_element_type=jnp.float32
    )
    d_keys = score_scale * jnp.einsum(
        "gts,tgd->sd", d_score, q_low, preferred_element_type=jnp.float32
    )
    d_values = jnp.einsum(
        "gts,tgd->sd", probs.astype(jnp.bfloat16), d_attn_heads, preferred_element_type=jnp.float32
    )
    d_q_f, grad_gain_query = query_pull(d_query)
    d_k_f, grad_gain_key = key_pull(d_keys[:, None, :])
    d_qkv = jnp.concatenate([d_q_f, d_k_f, d_values], axis=1).astype(jnp.bfloat16)
    normed1_term = jnp.einsum("tc,dc->td", d_qkv, own_weights, preferred_element_type=jnp.float32)
    grad_gain_one = (
        jnp.sum(normed1_term * first_normed.astype(jnp.float32), axis=0) / gain_one
    )
    normed1_low, sum_gate = lax.optimization_barrier(
        (normed1_term.astype(jnp.bfloat16), sum_gate)
    )
    d_normed1 = lax.psum_scatter(normed1_low, "dp", scatter_dimension=0, tiled=True)
    upper_low, d_normed1 = lax.optimization_barrier((grad_upper.astype(jnp.bfloat16), d_normed1))
    sum_upper = lax.psum_scatter(upper_low, "dp", scatter_dimension=1, tiled=True)
    d_tok_norm = norm1_pull(d_normed1.astype(jnp.float32))[0]
    grad_input = (d_resid + d_tok_norm)[None]
    sum_one, sum_query, sum_key, sum_two = lax.psum(
        (grad_gain_one, grad_gain_query, grad_gain_key, grad_gain_two), ("dp", "expert")
    )
    sum_gate = sum_gate.astype(jnp.float32)
    sum_upper = sum_upper.astype(jnp.float32)
    sum_down = sum_down.astype(jnp.float32)
    qkv_term = jnp.einsum("td,tc->dc", first_normed, d_qkv, preferred_element_type=jnp.float32)
    router_term = jnp.einsum("td,te->de", normed2, d_logits, preferred_element_type=jnp.float32)
    router_term = jnp.pad(router_term, ((0, 0), (0, head_dim - n_routed)))
    grad_blocks = (
        jnp.concatenate([qkv_term, router_term], axis=1)
        .astype(jnp.bfloat16)
        .reshape(n_dp, n_expert, w_rows, -1)
        .transpose(1, 0, 2, 3)
    )
    grad_blocks = lax.all_to_all(
        grad_blocks, "expert", split_axis=0, concat_axis=0, tiled=True
    ).astype(jnp.float32)
    grad_blocks = jnp.sum(grad_blocks, axis=0).astype(jnp.bfloat16)
    grad_blocks = lax.all_to_all(
        grad_blocks, "dp", split_axis=0, concat_axis=0, tiled=True
    ).astype(jnp.float32)

    def gather_heads(first):
        picked = grad_blocks[:, :, first : first + head_dim]
        picked = jnp.sum(picked.reshape(heads_kv, share, w_rows, head_dim), axis=1)
        return picked.transpose(1, 0, 2).reshape(w_rows, heads_kv * head_dim)

    sum_wq = grad_blocks[:, :, :q_cols].transpose(1, 0, 2).reshape(w_rows, heads_q * head_dim)
    sum_wk = gather_heads(q_cols)
    sum_wv = gather_heads(q_cols + head_dim)
    sum_wr = jnp.sum(grad_blocks[:, :, qkv_cols : qkv_cols + n_routed], axis=0)
    out_term = jnp.einsum("tc,td->cd", attn_low, all_branch, preferred_element_type=jnp.float32)
    out_term = lax.all_to_all(
        out_term.astype(jnp.bfloat16).reshape((n_expert,) + w_out.shape),
        "expert",
        split_axis=0,
        concat_axis=0,
        tiled=True,
    )
    sum_wo = jnp.sum(out_term.astype(jnp.float32), axis=0)
    return (
        output,
        grad_input,
        sum_one,
        sum_wq,
        sum_wk,
        sum_wv,
        sum_query,
        sum_key,
        sum_wo,
        sum_two,
        sum_wr,
        sum_gate,
        sum_upper,
        sum_down,
    )


def solution(mesh):
    return jax.shard_map(
        shards,
        mesh=mesh,
        in_specs=(
            P("expert", "dp", None),
            P(),
            P(("dp", "expert"), None),
            P(("dp", "expert"), None),
            P(("dp", "expert"), None),
            P(),
            P(),
            P(("dp", "expert"), None),
            P(),
            P(("dp", "expert"), None),
            P("expert", None, None),
            P("expert", None, None),
            P("expert", None, None),
            P("expert", "dp"),
            P("expert", "dp", None),
            P("expert", "dp", None),
        ),
        out_specs=(
            P("expert", "dp", None),
            P("expert", "dp", None),
            P(),
            P(("dp", "expert"), None),
            P(("dp", "expert"), None),
            P(("dp", "expert"), None),
            P(),
            P(),
            P(("dp", "expert"), None),
            P(),
            P(("dp", "expert"), None),
            P("expert", "dp", None),
            P("expert", "dp", None),
            P("expert", None, "dp"),
        ),
        check_vma=False,
    )
```

```python
import jax
import jax.numpy as jnp
from jax import lax
from jax.sharding import PartitionSpec as P

CAP = 48


EPSILON = 1e-06
THETA_BASE = 1000000.0
MASKED = -1e30


def norm_rows(values, gain):
    return values * lax.rsqrt(jnp.mean(values * values, axis=-1, keepdims=True) + EPSILON) * gain


def rotate_half(values):
    middle = values.shape[-1] // 2
    return jnp.concatenate([-values[..., middle:], values[..., :middle]], axis=-1)


def rope_tables(positions, head_width):
    freq_index = jnp.arange(head_width // 2).astype(jnp.float32)
    inverse = THETA_BASE ** (-2.0 * freq_index / head_width)
    angles = positions.astype(jnp.float32)[:, None] * inverse[None, :]
    angles = jnp.concatenate([angles, angles], axis=-1)
    return (jnp.cos(angles)[:, None, :], jnp.sin(angles)[:, None, :])


def prepare_heads(raw, gain, cosine_table, sine_table, heads):
    normed = norm_rows(raw.reshape(raw.shape[0], heads, -1), gain)
    return normed * cosine_table + rotate_half(normed) * sine_table


def silu_product(gate_pre, up_pre):
    return jax.nn.silu(gate_pre) * up_pre


def shards(
    tokens,
    norm1,
    w_query,
    key_projection,
    value_projection,
    q_gain,
    key_norm_gain,
    w_out,
    norm2,
    w_router,
    w_gate,
    w_up,
    w_down,
    segments,
    routes,
    grad_out,
):
    tok_in = tokens[0].astype(jnp.float32)
    tok_rows, model_dim = tok_in.shape
    head_dim = q_gain.shape[0]
    heads_q = w_query.shape[1] // head_dim
    heads_kv = key_projection.shape[1] // head_dim
    n_dp = lax.axis_size("dp")
    n_expert = lax.axis_size("expert")
    w_rows = w_query.shape[0]
    own_heads = heads_q // n_dp
    share = n_dp // heads_kv
    q_cols = own_heads * head_dim
    n_routed = w_router.shape[1]
    top_count = routes.shape[2]
    score_scale = head_dim ** (-0.5)
    gain_one = norm1.astype(jnp.float32)
    gain_two = norm2.astype(jnp.float32)
    gain_query = q_gain.astype(jnp.float32)
    gain_key = key_norm_gain.astype(jnp.float32)
    normed1_f, norm1_pull = jax.vjp(norm_rows, tok_in, gain_one)
    segment = lax.all_gather(segments[0].astype(jnp.bfloat16), "dp", axis=0, tiled=True)
    seq_rows = segment.shape[0]

    def spread_heads(matrix):
        return jnp.repeat(matrix.reshape(w_rows, heads_kv, head_dim), share, axis=1)

    router_pad = jnp.pad(w_router, ((0, 0), (0, head_dim - n_routed)))
    blocks = jnp.concatenate(
        [
            w_query.reshape(w_rows, n_dp, q_cols),
            spread_heads(key_projection),
            spread_heads(value_projection),
            jnp.broadcast_to(router_pad[:, None, :], (w_rows, n_dp, head_dim)),
        ],
        axis=2,
    ).transpose(1, 0, 2)
    blocks = lax.all_to_all(blocks, "dp", split_axis=0, concat_axis=0, tiled=True)
    first_normed, blocks = lax.optimization_barrier((normed1_f.astype(jnp.bfloat16), blocks))
    first_normed = lax.all_gather(first_normed, "dp", axis=0, tiled=True)

    def spread_expert(piece):
        copies = jnp.broadcast_to(piece[None], (n_expert,) + piece.shape)
        return lax.all_to_all(copies, "expert", split_axis=0, concat_axis=0, tiled=True)

    blocks, w_out = lax.optimization_barrier((spread_expert(blocks), w_out))
    own_weights = blocks.transpose(1, 0, 2, 3).reshape(model_dim, -1)
    qkv_cols = q_cols + 2 * head_dim
    full_router = own_weights[:, qkv_cols : qkv_cols + n_routed]
    own_weights = own_weights[:, :qkv_cols]
    own_out = spread_expert(w_out).reshape(q_cols, model_dim)
    raw = jnp.dot(first_normed, own_weights, preferred_element_type=jnp.float32)
    q_raw = raw[:, :q_cols]
    key_unrotated = raw[:, q_cols : q_cols + head_dim]
    value_low = raw[:, q_cols + head_dim :].astype(jnp.bfloat16)
    positions = jnp.arange(seq_rows, dtype=jnp.int32)
    cosine_table, sine_table = rope_tables(positions, head_dim)
    q_rot, query_pull = jax.vjp(
        lambda raw_in, gain_in: prepare_heads(raw_in, gain_in, cosine_table, sine_table, own_heads),
        q_raw,
        gain_query,
    )
    k_rot, key_pull = jax.vjp(
        lambda raw_in, gain_in: prepare_heads(raw_in, gain_in, cosine_table, sine_table, 1),
        key_unrotated,
        gain_key,
    )
    q_low = q_rot.astype(jnp.bfloat16)
    key_low = k_rot.astype(jnp.bfloat16).reshape(seq_rows, head_dim)
    allowed = (
        (positions[:, None] >= positions[None, :]) & (segment[:, None] == segment[None, :])
    )[None]

    def raw_weights():
        score = jnp.einsum("tgd,sd->gts", q_low, key_low, preferred_element_type=jnp.float32)
        return jnp.where(allowed, jnp.exp(score * score_scale), 0.0)

    weights = raw_weights()
    inverse_sum = 1.0 / jnp.sum(weights, axis=-1)
    attn_heads = (
        jnp.einsum(
            "gts,sd->gtd", weights.astype(jnp.bfloat16), value_low, preferred_element_type=jnp.float32
        )
        * inverse_sum[..., None]
    )
    attn_low = attn_heads.transpose(1, 0, 2).reshape(seq_rows, q_cols).astype(jnp.bfloat16)
    branch_term = jnp.dot(attn_low, own_out, preferred_element_type=jnp.float32)
    branch = lax.psum_scatter(
        branch_term.astype(jnp.bfloat16), "dp", scatter_dimension=0, tiled=True
    )
    residual = tok_in + branch.astype(jnp.float32)
    normed2_f, norm2_pull = jax.vjp(norm_rows, residual, gain_two)
    normed2 = normed2_f.astype(jnp.bfloat16)
    logits = jnp.dot(normed2, full_router, preferred_element_type=jnp.float32)
    chosen = routes[0]
    onehot = (chosen[:, :, None] == jnp.arange(n_routed, dtype=jnp.int32)).astype(jnp.float32)
    gate_probs = jax.nn.softmax(jnp.sum(onehot * logits[:, None, :], axis=2), axis=-1)
    flat_onehot = onehot.reshape(tok_rows * top_count, n_routed)
    route_index = jnp.arange(tok_rows * top_count, dtype=jnp.int32)
    earlier = (route_index[:, None] > route_index[None, :]).astype(jnp.bfloat16)
    counts = jnp.dot(earlier, flat_onehot.astype(jnp.bfloat16), preferred_element_type=jnp.float32)
    ranks = jnp.sum(counts * flat_onehot, axis=1).reshape(tok_rows, top_count)
    slots = chosen * CAP + ranks.astype(jnp.int32)
    slot_hits = slots[:, :, None] == jnp.arange(n_routed * CAP, dtype=jnp.int32)
    slot_gate = jnp.sum(jnp.where(slot_hits, gate_probs[:, :, None], 0.0), axis=(0, 1))
    route_picks = slot_hits.astype(jnp.bfloat16).transpose(1, 0, 2)
    token_picks = jnp.any(slot_hits, axis=1).astype(jnp.bfloat16)

    def to_slots(rows):
        return jnp.einsum("ts,td->sd", token_picks, rows, preferred_element_type=jnp.float32)

    send_rows = to_slots(normed2).astype(jnp.bfloat16).reshape(n_routed, CAP, model_dim)
    received = lax.all_to_all(send_rows, "expert", split_axis=0, concat_axis=1, tiled=True)
    gate_pre = jnp.einsum("erd,edf->erf", received, w_gate, preferred_element_type=jnp.float32)
    up_pre = jnp.einsum("erd,edf->erf", received, w_up, preferred_element_type=jnp.float32)
    hidden_f, act_pull = jax.vjp(silu_product, gate_pre, up_pre)
    hidden = hidden_f.astype(jnp.bfloat16)
    expert_out = jnp.einsum(
        "erf,efd->erd", hidden, w_down, preferred_element_type=jnp.float32
    ).astype(jnp.bfloat16)
    returned = lax.all_to_all(
        expert_out, "expert", split_axis=1, concat_axis=0, tiled=True
    ).reshape(n_routed * CAP, model_dim)
    route_out = jnp.einsum(
        "kts,sd->ktd", route_picks, returned, preferred_element_type=jnp.float32
    )
    mixture = jnp.sum(gate_probs.T[:, :, None] * route_out, axis=0)
    output = (residual + mixture).astype(jnp.bfloat16)[None]
    grad_rows = grad_out[0].astype(jnp.float32)
    d_gates = jnp.sum(grad_rows[None] * route_out, axis=-1).T
    d_picked = gate_probs * (d_gates - jnp.sum(gate_probs * d_gates, axis=1, keepdims=True))
    d_logits = jnp.sum(onehot * d_picked[:, :, None], axis=1).astype(jnp.bfloat16)
    d_send = (
        (slot_gate[:, None] * to_slots(grad_out[0]))
        .astype(jnp.bfloat16)
        .reshape(n_routed, CAP, model_dim)
    )
    d_recv = lax.all_to_all(d_send, "expert", split_axis=0, concat_axis=1, tiled=True)
    d_hidden = jnp.einsum("erd,efd->erf", d_recv, w_down, preferred_element_type=jnp.float32)
    grad_down = jnp.einsum("erf,erd->efd", hidden, d_recv, preferred_element_type=jnp.float32)
    d_gate_f, d_up_f = act_pull(d_hidden)
    d_gate = d_gate_f.astype(jnp.bfloat16)
    d_up = d_up_f.astype(jnp.bfloat16)
    grad_gate = jnp.einsum("erd,erf->edf", received, d_gate, preferred_element_type=jnp.float32)
    grad_upper = jnp.einsum("erd,erf->edf", received, d_up, preferred_element_type=jnp.float32)
    d_in = (
        jnp.einsum("erf,edf->erd", d_gate, w_gate, preferred_element_type=jnp.float32)
        + jnp.einsum("erf,edf->erd", d_up, w_up, preferred_element_type=jnp.float32)
    ).astype(jnp.bfloat16)
    d_back = lax.all_to_all(d_in, "expert", split_axis=1, concat_axis=0, tiled=True).reshape(
        n_routed * CAP, model_dim
    )
    d_normed2 = jnp.dot(token_picks, d_back, preferred_element_type=jnp.float32)
    d_normed2 = d_normed2 + jnp.einsum(
        "te,de->td", d_logits, full_router, preferred_element_type=jnp.float32
    )
    d_resid_norm, grad_gain_two = norm2_pull(d_normed2)
    d_resid = grad_rows + d_resid_norm
    sum_down = lax.psum_scatter(
        grad_down.astype(jnp.bfloat16), "dp", scatter_dimension=2, tiled=True
    )
    d_branch, sum_down = lax.optimization_barrier((d_resid.astype(jnp.bfloat16), sum_down))
    all_branch = lax.all_gather(d_branch, "dp", axis=0, tiled=True)
    gate_low, all_branch = lax.optimization_barrier((grad_gate.astype(jnp.bfloat16), all_branch))
    sum_gate = lax.psum_scatter(gate_low, "dp", scatter_dimension=1, tiled=True)
    d_attn = jnp.einsum(
        "td,cd->tc", all_branch, own_out, preferred_element_type=jnp.float32
    ).astype(jnp.bfloat16)
    d_attn_heads = d_attn.reshape(seq_rows, own_heads, head_dim)
    delta = jnp.sum(d_attn_heads.transpose(1, 0, 2).astype(jnp.float32) * attn_heads, axis=-1)
    probs = raw_weights() * inverse_sum[..., None]
    d_probs = jnp.einsum(
        "tgd,sd->gts", d_attn_heads, value_low, preferred_element_type=jnp.float32
    )
    d_score = (probs * (d_probs - delta[..., None])).astype(jnp.bfloat16)
    d_query = score_scale * jnp.einsum(
        "gts,sd->tgd", d_score, key_low, preferred_element_type=jnp.float32
    )
    d_keys = score_scale * jnp.einsum(
        "gts,tgd->sd", d_score, q_low, preferred_element_type=jnp.float32
    )
    d_values = jnp.einsum(
        "gts,tgd->sd", probs.astype(jnp.bfloat16), d_attn_heads, preferred_element_type=jnp.float32
    )
    d_q_f, grad_gain_query = query_pull(d_query)
    d_k_f, grad_gain_key = key_pull(d_keys[:, None, :])
    d_qkv = jnp.concatenate([d_q_f, d_k_f, d_values], axis=1).astype(jnp.bfloat16)
    out_term = jnp.einsum("tc,td->cd", attn_low, all_branch, preferred_element_type=jnp.float32)
    out_term = lax.all_to_all(
        out_term.astype(jnp.bfloat16).reshape((n_expert,) + w_out.shape),
        "expert",
        split_axis=0,
        concat_axis=0,
        tiled=True,
    )
    normed1_term = jnp.einsum("tc,dc->td", d_qkv, own_weights, preferred_element_type=jnp.float32)
    grad_gain_one = (
        jnp.sum(normed1_term * first_normed.astype(jnp.float32), axis=0) / gain_one
    )
    normed1_low, sum_gate, out_term = lax.optimization_barrier(
        (normed1_term.astype(jnp.bfloat16), sum_gate, out_term)
    )
    d_normed1 = lax.psum_scatter(normed1_low, "dp", scatter_dimension=0, tiled=True)
    qkv_term = jnp.einsum("td,tc->dc", first_normed, d_qkv, preferred_element_type=jnp.float32)
    router_term = jnp.einsum("td,te->de", normed2, d_logits, preferred_element_type=jnp.float32)
    router_term = jnp.pad(router_term, ((0, 0), (0, head_dim - n_routed)))
    grad_blocks = (
        jnp.concatenate([qkv_term, router_term], axis=1)
        .astype(jnp.bfloat16)
        .reshape(n_dp, n_expert, w_rows, -1)
        .transpose(1, 0, 2, 3)
    )
    grad_blocks = lax.all_to_all(grad_blocks, "expert", split_axis=0, concat_axis=0, tiled=True)
    gain_terms = (grad_gain_one, grad_gain_query, grad_gain_key, grad_gain_two)
    upper_low, d_normed1, grad_blocks, gain_terms = lax.optimization_barrier(
        (grad_upper.astype(jnp.bfloat16), d_normed1, grad_blocks, gain_terms)
    )
    sum_upper = lax.psum_scatter(upper_low, "dp", scatter_dimension=1, tiled=True)
    d_tok_norm = norm1_pull(d_normed1.astype(jnp.float32))[0]
    grad_input = (d_resid + d_tok_norm)[None]
    sum_one, sum_query, sum_key, sum_two = lax.psum(gain_terms, ("dp", "expert"))
    sum_gate = sum_gate.astype(jnp.float32)
    sum_upper = sum_upper.astype(jnp.float32)
    sum_down = sum_down.astype(jnp.float32)
    grad_blocks = jnp.sum(grad_blocks.astype(jnp.float32), axis=0).astype(jnp.bfloat16)
    grad_blocks = lax.all_to_all(
        grad_blocks, "dp", split_axis=0, concat_axis=0, tiled=True
    ).astype(jnp.float32)

    def gather_heads(first):
        picked = grad_blocks[:, :, first : first + head_dim]
        picked = jnp.sum(picked.reshape(heads_kv, share, w_rows, head_dim), axis=1)
        return picked.transpose(1, 0, 2).reshape(w_rows, heads_kv * head_dim)

    sum_wq = grad_blocks[:, :, :q_cols].transpose(1, 0, 2).reshape(w_rows, heads_q * head_dim)
    sum_wk = gather_heads(q_cols)
    sum_wv = gather_heads(q_cols + head_dim)
    sum_wr = jnp.sum(grad_blocks[:, :, qkv_cols : qkv_cols + n_routed], axis=0)
    sum_wo = jnp.sum(out_term.astype(jnp.float32), axis=0)
    return (
        output,
        grad_input,
        sum_one,
        sum_wq,
        sum_wk,
        sum_wv,
        sum_query,
        sum_key,
        sum_wo,
        sum_two,
        sum_wr,
        sum_gate,
        sum_upper,
        sum_down,
    )


def solution(mesh):
    return jax.shard_map(
        shards,
        mesh=mesh,
        in_specs=(
            P("expert", "dp", None),
            P(),
            P(("dp", "expert"), None),
            P(("dp", "expert"), None),
            P(("dp", "expert"), None),
            P(),
            P(),
            P(("dp", "expert"), None),
            P(),
            P(("dp", "expert"), None),
            P("expert", None, None),
            P("expert", None, None),
            P("expert", None, None),
            P("expert", "dp"),
            P("expert", "dp", None),
            P("expert", "dp", None),
        ),
        out_specs=(
            P("expert", "dp", None),
            P("expert", "dp", None),
            P(),
            P(("dp", "expert"), None),
            P(("dp", "expert"), None),
            P(("dp", "expert"), None),
            P(),
            P(),
            P(("dp", "expert"), None),
            P(),
            P(("dp", "expert"), None),
            P("expert", "dp", None),
            P("expert", "dp", None),
            P("expert", None, "dp"),
        ),
        check_vma=False,
    )
```

```python
import jax
import jax.numpy as jnp
from jax import lax
from jax.sharding import PartitionSpec as P

CAP = 48
DP = ("outer", "core")


EPSILON = 1e-06
THETA_BASE = 1000000.0
MASKED = -1e30


def norm_rows(values, gain):
    return values * lax.rsqrt(jnp.mean(values * values, axis=-1, keepdims=True) + EPSILON) * gain


def rotate_half(values):
    middle = values.shape[-1] // 2
    return jnp.concatenate([-values[..., middle:], values[..., :middle]], axis=-1)


def rope_tables(positions, head_width):
    freq_index = jnp.arange(head_width // 2).astype(jnp.float32)
    inverse = THETA_BASE ** (-2.0 * freq_index / head_width)
    angles = positions.astype(jnp.float32)[:, None] * inverse[None, :]
    angles = jnp.concatenate([angles, angles], axis=-1)
    return (jnp.cos(angles)[:, None, :], jnp.sin(angles)[:, None, :])


def prepare_heads(raw, gain, cosine_table, sine_table, heads):
    normed = norm_rows(raw.reshape(raw.shape[0], heads, -1), gain)
    return normed * cosine_table + rotate_half(normed) * sine_table


def silu_product(gate_pre, up_pre):
    return jax.nn.silu(gate_pre) * up_pre


def own_and_other(values, axis):
    size = values.shape[axis] // lax.axis_size(DP)
    split = values.shape[:axis] + (-1, 2, size) + values.shape[axis + 1 :]
    merged = values.shape[:axis] + (-1,) + values.shape[axis + 1 :]
    split_values = values.reshape(split)
    core = lax.axis_index("core")

    def pick(index):
        part = lax.dynamic_index_in_dim(split_values, index, axis + 1, keepdims=False)
        return part.reshape(merged)

    return (pick(core), pick(1 - core))


def add_pair(own, other):
    arrived = lax.ppermute(other.astype(jnp.bfloat16), "core", [(0, 1), (1, 0)])
    return (own + arrived.astype(jnp.float32)).astype(jnp.bfloat16)


def expert_term(columns, weights):
    own, other = own_and_other(columns, 2)
    return add_pair(
        jnp.einsum("erd,erf->edf", own, weights, preferred_element_type=jnp.float32),
        jnp.einsum("erd,erf->edf", other, weights, preferred_element_type=jnp.float32),
    )


def slot_table(chosen, n_routed):
    rows, top_count = chosen.shape[-2:]
    flat = chosen.reshape(-1, rows * top_count)
    onehot = (flat[:, :, None] == jnp.arange(n_routed, dtype=jnp.int32)).astype(jnp.float32)
    index = jnp.arange(rows * top_count, dtype=jnp.int32)
    earlier = (index[:, None] > index[None, :]).astype(jnp.bfloat16)
    counts = jnp.einsum(
        "ij,sje->sie", earlier, onehot.astype(jnp.bfloat16), preferred_element_type=jnp.float32
    )
    ranks = jnp.sum(counts * onehot, axis=2).astype(jnp.int32)
    return (flat * CAP + ranks).reshape(chosen.shape)


def choose_gates(normed, router, chosen):
    logits = jnp.dot(normed, router, preferred_element_type=jnp.float32)
    experts = jnp.arange(router.shape[1], dtype=jnp.int32)
    onehot = (chosen[:, :, None] == experts).astype(jnp.float32)
    return (jax.nn.softmax(jnp.sum(onehot * logits[:, None, :], axis=2), axis=-1), onehot)


def shards(
    tokens,
    norm1,
    w_query,
    key_projection,
    value_projection,
    q_gain,
    key_norm_gain,
    w_out,
    norm2,
    w_router,
    w_gate,
    w_up,
    w_down,
    segments,
    routes,
    grad_out,
):
    tok_in = tokens[0].astype(jnp.float32)
    tok_rows, model_dim = tok_in.shape
    head_dim = q_gain.shape[0]
    heads_q = w_query.shape[1] // head_dim
    heads_kv = key_projection.shape[1] // head_dim
    n_dp = lax.axis_size(DP)
    n_expert = lax.axis_size("expert")
    w_rows = w_query.shape[0]
    own_heads = heads_q // n_dp
    share = n_dp // heads_kv
    q_cols = own_heads * head_dim
    n_routed = w_router.shape[1]
    top_count = routes.shape[2]
    score_scale = head_dim ** (-0.5)
    gain_one = norm1.astype(jnp.float32)
    gain_two = norm2.astype(jnp.float32)
    gain_query = q_gain.astype(jnp.float32)
    gain_key = key_norm_gain.astype(jnp.float32)
    normed1_f, norm1_pull = jax.vjp(norm_rows, tok_in, gain_one)
    segment = lax.all_gather(segments[0].astype(jnp.bfloat16), DP, axis=0, tiled=True)
    seq_rows = segment.shape[0]

    def spread_heads(matrix):
        return jnp.repeat(matrix.reshape(w_rows, heads_kv, head_dim), share, axis=1)

    router_pad = jnp.pad(w_router, ((0, 0), (0, head_dim - n_routed)))
    blocks = jnp.concatenate(
        [
            w_query.reshape(w_rows, n_dp, q_cols),
            spread_heads(key_projection),
            spread_heads(value_projection),
            jnp.broadcast_to(router_pad[:, None, :], (w_rows, n_dp, head_dim)),
        ],
        axis=2,
    ).transpose(1, 0, 2)
    blocks = lax.all_to_all(blocks, DP, split_axis=0, concat_axis=0, tiled=True)

    def spread_expert(piece):
        copies = jnp.broadcast_to(piece[None], (n_expert,) + piece.shape)
        return lax.all_to_all(copies, "expert", split_axis=0, concat_axis=0, tiled=True)

    all_grad = spread_expert(grad_out[0])
    first_normed, blocks, all_grad = lax.optimization_barrier(
        (normed1_f.astype(jnp.bfloat16), blocks, all_grad)
    )
    first_normed = lax.all_gather(first_normed, DP, axis=0, tiled=True)
    all_routes = lax.all_gather(routes[0], "expert", axis=0)
    blocks, w_out = lax.optimization_barrier((spread_expert(blocks), w_out))
    own_weights = blocks.transpose(1, 0, 2, 3).reshape(model_dim, -1)
    qkv_cols = q_cols + 2 * head_dim
    full_router = own_weights[:, qkv_cols : qkv_cols + n_routed]
    own_weights = own_weights[:, :qkv_cols]
    own_out = spread_expert(w_out).reshape(q_cols, model_dim)
    raw = jnp.dot(first_normed, own_weights, preferred_element_type=jnp.float32)
    q_raw = raw[:, :q_cols]
    key_unrotated = raw[:, q_cols : q_cols + head_dim]
    value_low = raw[:, q_cols + head_dim :].astype(jnp.bfloat16)
    positions = jnp.arange(seq_rows, dtype=jnp.int32)
    cosine_table, sine_table = rope_tables(positions, head_dim)
    q_rot, query_pull = jax.vjp(
        lambda raw_in, gain_in: prepare_heads(raw_in, gain_in, cosine_table, sine_table, own_heads),
        q_raw,
        gain_query,
    )
    k_rot, key_pull = jax.vjp(
        lambda raw_in, gain_in: prepare_heads(raw_in, gain_in, cosine_table, sine_table, 1),
        key_unrotated,
        gain_key,
    )
    q_low = q_rot.astype(jnp.bfloat16)
    key_low = k_rot.astype(jnp.bfloat16).reshape(seq_rows, head_dim)
    allowed = (
        (positions[:, None] >= positions[None, :]) & (segment[:, None] == segment[None, :])
    )[None]

    def raw_weights():
        score = jnp.einsum("tgd,sd->gts", q_low, key_low, preferred_element_type=jnp.float32)
        return jnp.where(allowed, jnp.exp(score * score_scale), 0.0)

    weights = raw_weights()
    inverse_sum = 1.0 / jnp.sum(weights, axis=-1)
    attn_heads = (
        jnp.einsum(
            "gts,sd->gtd", weights.astype(jnp.bfloat16), value_low, preferred_element_type=jnp.float32
        )
        * inverse_sum[..., None]
    )
    attn_low = attn_heads.transpose(1, 0, 2).reshape(seq_rows, q_cols).astype(jnp.bfloat16)
    branch_term = jnp.dot(attn_low, own_out, preferred_element_type=jnp.float32)
    branch = lax.psum_scatter(
        branch_term.astype(jnp.bfloat16), DP, scatter_dimension=0, tiled=True
    )
    residual = tok_in + branch.astype(jnp.float32)
    normed2_f, norm2_pull = jax.vjp(norm_rows, residual, gain_two)
    normed2 = normed2_f.astype(jnp.bfloat16)
    all_normed = spread_expert(normed2)
    chosen = routes[0]
    gate_probs, onehot = choose_gates(normed2, full_router, chosen)
    slot_count = n_routed * CAP
    slots = slot_table(chosen, n_routed)
    slot_hits = slots[:, :, None] == jnp.arange(slot_count, dtype=jnp.int32)
    route_picks = slot_hits.astype(jnp.bfloat16).transpose(1, 0, 2)
    token_picks = jnp.any(slot_hits, axis=1).astype(jnp.bfloat16)
    held = w_gate.shape[0]
    first_slot = lax.axis_index("expert") * (held * CAP)
    all_hits = (slot_table(all_routes, n_routed) - first_slot)[..., None] == jnp.arange(
        held * CAP, dtype=jnp.int32
    )
    all_picks = jnp.any(all_hits, axis=2).astype(jnp.bfloat16)

    def to_slots(rows):
        return jnp.einsum("stl,std->sld", all_picks, rows, preferred_element_type=jnp.float32)

    def by_expert(rows):
        rows = rows.reshape(n_expert, held, CAP, model_dim).transpose(1, 0, 2, 3)
        return rows.reshape(held, n_expert * CAP, model_dim)

    all_gates, _ = choose_gates(
        all_normed.reshape(-1, model_dim), full_router, all_routes.reshape(-1, top_count)
    )
    all_gates = all_gates.reshape(all_routes.shape)
    slot_gate = jnp.sum(jnp.where(all_hits, all_gates[..., None], 0.0), axis=(1, 2))
    received = by_expert(to_slots(all_normed).astype(jnp.bfloat16))
    d_recv = by_expert((slot_gate[:, :, None] * to_slots(all_grad)).astype(jnp.bfloat16))
    gate_pre = jnp.einsum("erd,edf->erf", received, w_gate, preferred_element_type=jnp.float32)
    up_pre = jnp.einsum("erd,edf->erf", received, w_up, preferred_element_type=jnp.float32)
    hidden_f, act_pull = jax.vjp(silu_product, gate_pre, up_pre)
    hidden = hidden_f.astype(jnp.bfloat16)
    expert_out = jnp.einsum(
        "erf,efd->erd", hidden, w_down, preferred_element_type=jnp.float32
    ).astype(jnp.bfloat16)
    returned = lax.all_to_all(
        expert_out, "expert", split_axis=1, concat_axis=0, tiled=True
    ).reshape(n_routed * CAP, model_dim)
    route_out = jnp.einsum(
        "kts,sd->ktd", route_picks, returned, preferred_element_type=jnp.float32
    )
    mixture = jnp.sum(gate_probs.T[:, :, None] * route_out, axis=0)
    output = (residual + mixture).astype(jnp.bfloat16)[None]
    grad_rows = grad_out[0].astype(jnp.float32)
    d_gates = jnp.sum(grad_rows[None] * route_out, axis=-1).T
    d_picked = gate_probs * (d_gates - jnp.sum(gate_probs * d_gates, axis=1, keepdims=True))
    d_logits = jnp.sum(onehot * d_picked[:, :, None], axis=1).astype(jnp.bfloat16)
    d_hidden = jnp.einsum("erd,efd->erf", d_recv, w_down, preferred_element_type=jnp.float32)
    grad_down = expert_term(d_recv, hidden)
    d_gate_f, d_up_f = act_pull(d_hidden)
    d_gate = d_gate_f.astype(jnp.bfloat16)
    d_up = d_up_f.astype(jnp.bfloat16)
    grad_gate = expert_term(received, d_gate)
    grad_upper = expert_term(received, d_up)
    d_in = (
        jnp.einsum("erf,edf->erd", d_gate, w_gate, preferred_element_type=jnp.float32)
        + jnp.einsum("erf,edf->erd", d_up, w_up, preferred_element_type=jnp.float32)
    ).astype(jnp.bfloat16)
    d_back = lax.all_to_all(d_in, "expert", split_axis=1, concat_axis=0, tiled=True).reshape(
        n_routed * CAP, model_dim
    )
    d_normed2 = jnp.dot(token_picks, d_back, preferred_element_type=jnp.float32)
    d_normed2 = d_normed2 + jnp.einsum(
        "te,de->td", d_logits, full_router, preferred_element_type=jnp.float32
    )
    d_resid_norm, grad_gain_two = norm2_pull(d_normed2)
    d_resid = grad_rows + d_resid_norm
    sum_down = lax.psum_scatter(grad_down, "outer", scatter_dimension=1, tiled=True)
    d_branch, sum_down = lax.optimization_barrier((d_resid.astype(jnp.bfloat16), sum_down))
    all_branch = lax.all_gather(d_branch, DP, axis=0, tiled=True)
    gate_low, all_branch = lax.optimization_barrier((grad_gate, all_branch))
    sum_gate = lax.psum_scatter(gate_low, "outer", scatter_dimension=1, tiled=True)
    d_attn = jnp.einsum(
        "td,cd->tc", all_branch, own_out, preferred_element_type=jnp.float32
    ).astype(jnp.bfloat16)
    d_attn_heads = d_attn.reshape(seq_rows, own_heads, head_dim)
    delta = jnp.sum(d_attn_heads.transpose(1, 0, 2).astype(jnp.float32) * attn_heads, axis=-1)
    probs = raw_weights() * inverse_sum[..., None]
    d_probs = jnp.einsum(
        "tgd,sd->gts", d_attn_heads, value_low, preferred_element_type=jnp.float32
    )
    d_score = (probs * (d_probs - delta[..., None])).astype(jnp.bfloat16)
    d_query = score_scale * jnp.einsum(
        "gts,sd->tgd", d_score, key_low, preferred_element_type=jnp.float32
    )
    d_keys = score_scale * jnp.einsum(
        "gts,tgd->sd", d_score, q_low, preferred_element_type=jnp.float32
    )
    d_values = jnp.einsum(
        "gts,tgd->sd", probs.astype(jnp.bfloat16), d_attn_heads, preferred_element_type=jnp.float32
    )
    d_q_f, grad_gain_query = query_pull(d_query)
    d_k_f, grad_gain_key = key_pull(d_keys[:, None, :])
    d_qkv = jnp.concatenate([d_q_f, d_k_f, d_values], axis=1).astype(jnp.bfloat16)
    out_term = jnp.einsum("tc,td->cd", attn_low, all_branch, preferred_element_type=jnp.float32)
    out_term = lax.all_to_all(
        out_term.astype(jnp.bfloat16).reshape((n_expert,) + w_out.shape),
        "expert",
        split_axis=0,
        concat_axis=0,
        tiled=True,
    )
    normed1_own, normed1_other = (
        jnp.einsum("tc,dc->td", part, own_weights, preferred_element_type=jnp.float32)
        for part in own_and_other(d_qkv, 0)
    )
    rows_own, rows_other = own_and_other(first_normed, 0)
    grad_gain_one = (
        jnp.sum(normed1_own * rows_own.astype(jnp.float32), axis=0)
        + jnp.sum(normed1_other * rows_other.astype(jnp.float32), axis=0)
    ) / gain_one
    normed1_low, sum_gate, out_term = lax.optimization_barrier(
        (add_pair(normed1_own, normed1_other), sum_gate, out_term)
    )
    d_normed1 = lax.psum_scatter(normed1_low, "outer", scatter_dimension=0, tiled=True)
    qkv_term = jnp.einsum("td,tc->dc", first_normed, d_qkv, preferred_element_type=jnp.float32)
    router_term = jnp.einsum("td,te->de", normed2, d_logits, preferred_element_type=jnp.float32)
    router_term = jnp.pad(router_term, ((0, 0), (0, head_dim - n_routed)))
    grad_blocks = (
        jnp.concatenate([qkv_term, router_term], axis=1)
        .astype(jnp.bfloat16)
        .reshape(n_dp, n_expert, w_rows, -1)
        .transpose(1, 0, 2, 3)
    )
    grad_blocks = lax.all_to_all(grad_blocks, "expert", split_axis=0, concat_axis=0, tiled=True)
    gain_terms = (grad_gain_one, grad_gain_query, grad_gain_key, grad_gain_two)
    upper_low, d_normed1, grad_blocks, gain_terms = lax.optimization_barrier(
        (grad_upper, d_normed1, grad_blocks, gain_terms)
    )
    sum_upper = lax.psum_scatter(upper_low, "outer", scatter_dimension=1, tiled=True)
    d_tok_norm = norm1_pull(d_normed1.astype(jnp.float32))[0]
    grad_input = (d_resid + d_tok_norm)[None]
    sum_one, sum_query, sum_key, sum_two = lax.psum(gain_terms, (*DP, "expert"))
    sum_gate = sum_gate.astype(jnp.float32)
    sum_upper = sum_upper.astype(jnp.float32)
    sum_down = sum_down.astype(jnp.float32).transpose(0, 2, 1)
    grad_blocks = jnp.sum(grad_blocks.astype(jnp.float32), axis=0).astype(jnp.bfloat16)
    grad_blocks = lax.all_to_all(
        grad_blocks, DP, split_axis=0, concat_axis=0, tiled=True
    ).astype(jnp.float32)

    def gather_heads(first):
        picked = grad_blocks[:, :, first : first + head_dim]
        picked = jnp.sum(picked.reshape(heads_kv, share, w_rows, head_dim), axis=1)
        return picked.transpose(1, 0, 2).reshape(w_rows, heads_kv * head_dim)

    sum_wq = grad_blocks[:, :, :q_cols].transpose(1, 0, 2).reshape(w_rows, heads_q * head_dim)
    sum_wk = gather_heads(q_cols)
    sum_wv = gather_heads(q_cols + head_dim)
    sum_wr = jnp.sum(grad_blocks[:, :, qkv_cols : qkv_cols + n_routed], axis=0)
    sum_wo = jnp.sum(out_term.astype(jnp.float32), axis=0)
    return (
        output,
        grad_input,
        sum_one,
        sum_wq,
        sum_wk,
        sum_wv,
        sum_query,
        sum_key,
        sum_wo,
        sum_two,
        sum_wr,
        sum_gate,
        sum_upper,
        sum_down,
    )


def solution(mesh):
    n_dp, n_expert = mesh.devices.shape
    view = jax.sharding.Mesh(
        mesh.devices.reshape(n_dp // 2, 2, n_expert), ("outer", "core", "expert")
    )
    rows = P((*DP, "expert"), None)
    return jax.shard_map(
        shards,
        mesh=view,
        in_specs=(
            P("expert", DP, None),
            P(),
            rows,
            rows,
            rows,
            P(),
            P(),
            rows,
            P(),
            rows,
            P("expert", None, None),
            P("expert", None, None),
            P("expert", None, None),
            P("expert", DP),
            P("expert", DP, None),
            P("expert", DP, None),
        ),
        out_specs=(
            P("expert", DP, None),
            P("expert", DP, None),
            P(),
            rows,
            rows,
            rows,
            P(),
            P(),
            rows,
            P(),
            rows,
            P("expert", DP, None),
            P("expert", DP, None),
            P("expert", None, DP),
        ),
        check_vma=False,
    )
```

```python
import jax
import jax.numpy as jnp
from jax import lax
from jax.sharding import PartitionSpec as P

CAP = 48
DP = ("outer", "core")


EPSILON = 1e-06
THETA_BASE = 1000000.0
MASKED = -1e30


def norm_rows(values, gain):
    return values * lax.rsqrt(jnp.mean(values * values, axis=-1, keepdims=True) + EPSILON) * gain


def rotate_half(values):
    middle = values.shape[-1] // 2
    return jnp.concatenate([-values[..., middle:], values[..., :middle]], axis=-1)


def rope_tables(positions, head_width):
    freq_index = jnp.arange(head_width // 2).astype(jnp.float32)
    inverse = THETA_BASE ** (-2.0 * freq_index / head_width)
    angles = positions.astype(jnp.float32)[:, None] * inverse[None, :]
    angles = jnp.concatenate([angles, angles], axis=-1)
    return (jnp.cos(angles)[:, None, :], jnp.sin(angles)[:, None, :])


def prepare_heads(raw, gain, cosine_table, sine_table, heads):
    normed = norm_rows(raw.reshape(raw.shape[0], heads, -1), gain)
    return normed * cosine_table + rotate_half(normed) * sine_table


def silu_product(gate_pre, up_pre):
    return jax.nn.silu(gate_pre) * up_pre


def pair_sum(values, axis):
    values = values.astype(jnp.bfloat16)
    size = values.shape[axis] // lax.axis_size(DP)
    split = values.shape[:axis] + (-1, 2, size) + values.shape[axis + 1 :]
    merged = values.shape[:axis] + (-1,) + values.shape[axis + 1 :]
    core = lax.axis_index("core")

    def pick(index):
        return lax.dynamic_index_in_dim(values.reshape(split), index, axis + 1, keepdims=False)

    arrived = lax.ppermute(pick(1 - core), "core", [(0, 1), (1, 0)])
    total = pick(core).astype(jnp.float32) + arrived.astype(jnp.float32)
    return total.astype(jnp.bfloat16).reshape(merged)


def expert_term(rows, weights):
    return pair_sum(
        jnp.einsum("erd,erf->edf", rows, weights, preferred_element_type=jnp.float32), 1
    )


def slot_table(chosen, n_routed):
    rows, top_count = chosen.shape[-2:]
    flat = chosen.reshape(-1, rows * top_count)
    onehot = (flat[:, :, None] == jnp.arange(n_routed, dtype=jnp.int32)).astype(jnp.float32)
    index = jnp.arange(rows * top_count, dtype=jnp.int32)
    earlier = (index[:, None] > index[None, :]).astype(jnp.bfloat16)
    counts = jnp.einsum(
        "ij,sje->sie", earlier, onehot.astype(jnp.bfloat16), preferred_element_type=jnp.float32
    )
    ranks = jnp.sum(counts * onehot, axis=2).astype(jnp.int32)
    return (flat * CAP + ranks).reshape(chosen.shape)


def choose_gates(normed, router, chosen):
    logits = jnp.dot(normed, router, preferred_element_type=jnp.float32)
    experts = jnp.arange(router.shape[1], dtype=jnp.int32)
    onehot = (chosen[:, :, None] == experts).astype(jnp.float32)
    return (jax.nn.softmax(jnp.sum(onehot * logits[:, None, :], axis=2), axis=-1), onehot)


def shards(
    tokens,
    norm1,
    w_query,
    key_projection,
    value_projection,
    q_gain,
    key_norm_gain,
    w_out,
    norm2,
    w_router,
    w_gate,
    w_up,
    w_down,
    segments,
    routes,
    grad_out,
):
    tok_in = tokens[0].astype(jnp.float32)
    tok_rows, model_dim = tok_in.shape
    head_dim = q_gain.shape[0]
    heads_q = w_query.shape[1] // head_dim
    heads_kv = key_projection.shape[1] // head_dim
    n_dp = lax.axis_size(DP)
    n_expert = lax.axis_size("expert")
    w_rows = w_query.shape[0]
    own_heads = heads_q // n_dp
    share = n_dp // heads_kv
    q_cols = own_heads * head_dim
    n_routed = w_router.shape[1]
    top_count = routes.shape[2]
    score_scale = head_dim ** (-0.5)
    gain_one = norm1.astype(jnp.float32)
    gain_two = norm2.astype(jnp.float32)
    gain_query = q_gain.astype(jnp.float32)
    gain_key = key_norm_gain.astype(jnp.float32)
    normed1_f, norm1_pull = jax.vjp(norm_rows, tok_in, gain_one)
    segment = lax.all_gather(segments[0].astype(jnp.bfloat16), DP, axis=0, tiled=True)
    seq_rows = segment.shape[0]

    def spread_heads(matrix):
        return jnp.repeat(matrix.reshape(w_rows, heads_kv, head_dim), share, axis=1)

    router_pad = jnp.pad(w_router, ((0, 0), (0, head_dim - n_routed)))
    blocks = jnp.concatenate(
        [
            w_query.reshape(w_rows, n_dp, q_cols),
            spread_heads(key_projection),
            spread_heads(value_projection),
            jnp.broadcast_to(router_pad[:, None, :], (w_rows, n_dp, head_dim)),
        ],
        axis=2,
    ).transpose(1, 0, 2)
    blocks = lax.all_to_all(blocks, DP, split_axis=0, concat_axis=0, tiled=True)

    def spread_expert(piece):
        copies = jnp.broadcast_to(piece[None], (n_expert,) + piece.shape)
        return lax.all_to_all(copies, "expert", split_axis=0, concat_axis=0, tiled=True)

    first_normed, blocks = lax.optimization_barrier((normed1_f.astype(jnp.bfloat16), blocks))
    first_normed = lax.all_gather(first_normed, DP, axis=0, tiled=True)
    all_routes = lax.all_gather(routes[0], "expert", axis=0)
    blocks, w_out, all_routes, segment = lax.optimization_barrier(
        (spread_expert(blocks), w_out, all_routes, segment)
    )
    own_weights = blocks.transpose(1, 0, 2, 3).reshape(model_dim, -1)
    qkv_cols = q_cols + 2 * head_dim
    full_router = own_weights[:, qkv_cols : qkv_cols + n_routed]
    own_weights = own_weights[:, :qkv_cols]
    own_out = spread_expert(w_out).reshape(q_cols, model_dim)
    raw = jnp.dot(first_normed, own_weights, preferred_element_type=jnp.float32)
    q_raw = raw[:, :q_cols]
    key_unrotated = raw[:, q_cols : q_cols + head_dim]
    value_low = raw[:, q_cols + head_dim :].astype(jnp.bfloat16)
    positions = jnp.arange(seq_rows, dtype=jnp.int32)
    cosine_table, sine_table = rope_tables(positions, head_dim)
    q_rot, query_pull = jax.vjp(
        lambda raw_in, gain_in: prepare_heads(raw_in, gain_in, cosine_table, sine_table, own_heads),
        q_raw,
        gain_query,
    )
    k_rot, key_pull = jax.vjp(
        lambda raw_in, gain_in: prepare_heads(raw_in, gain_in, cosine_table, sine_table, 1),
        key_unrotated,
        gain_key,
    )
    q_low = q_rot.astype(jnp.bfloat16)
    key_low = k_rot.astype(jnp.bfloat16).reshape(seq_rows, head_dim)
    allowed = (
        (positions[:, None] >= positions[None, :]) & (segment[:, None] == segment[None, :])
    )[None]

    def raw_weights():
        score = jnp.einsum("tgd,sd->gts", q_low, key_low, preferred_element_type=jnp.float32)
        return jnp.where(allowed, jnp.exp(score * score_scale), 0.0)

    weights = raw_weights()
    inverse_sum = 1.0 / jnp.sum(weights, axis=-1)
    attn_heads = (
        jnp.einsum(
            "gts,sd->gtd", weights.astype(jnp.bfloat16), value_low, preferred_element_type=jnp.float32
        )
        * inverse_sum[..., None]
    )
    attn_low = attn_heads.transpose(1, 0, 2).reshape(seq_rows, q_cols).astype(jnp.bfloat16)
    branch_term = jnp.dot(attn_low, own_out, preferred_element_type=jnp.float32)
    branch_low, late_grad = lax.optimization_barrier((branch_term.astype(jnp.bfloat16), grad_out[0]))
    branch = lax.psum_scatter(branch_low, DP, scatter_dimension=0, tiled=True)
    branch, all_grad = lax.optimization_barrier((branch, spread_expert(late_grad)))
    residual = tok_in + branch.astype(jnp.float32)
    normed2_f, norm2_pull = jax.vjp(norm_rows, residual, gain_two)
    normed2 = normed2_f.astype(jnp.bfloat16)
    all_normed = spread_expert(normed2)
    chosen = routes[0]
    gate_probs, onehot = choose_gates(normed2, full_router, chosen)
    slot_count = n_routed * CAP
    slots = slot_table(chosen, n_routed)
    slot_hits = slots[:, :, None] == jnp.arange(slot_count, dtype=jnp.int32)
    route_picks = slot_hits.astype(jnp.bfloat16).transpose(1, 0, 2)
    token_picks = jnp.any(slot_hits, axis=1).astype(jnp.bfloat16)
    held = w_gate.shape[0]
    first_slot = lax.axis_index("expert") * (held * CAP)
    all_hits = (slot_table(all_routes, n_routed) - first_slot)[..., None] == jnp.arange(
        held * CAP, dtype=jnp.int32
    )
    all_picks = jnp.any(all_hits, axis=2).astype(jnp.bfloat16)

    def to_slots(rows):
        return jnp.einsum("stl,std->sld", all_picks, rows, preferred_element_type=jnp.float32)

    def by_expert(rows):
        rows = rows.reshape(n_expert, held, CAP, model_dim).transpose(1, 0, 2, 3)
        return rows.reshape(held, n_expert * CAP, model_dim)

    all_gates, _ = choose_gates(
        all_normed.reshape(-1, model_dim), full_router, all_routes.reshape(-1, top_count)
    )
    all_gates = all_gates.reshape(all_routes.shape)
    slot_gate = jnp.sum(jnp.where(all_hits, all_gates[..., None], 0.0), axis=(1, 2))
    received = by_expert(to_slots(all_normed).astype(jnp.bfloat16))
    d_recv = by_expert((slot_gate[:, :, None] * to_slots(all_grad)).astype(jnp.bfloat16))
    gate_pre = jnp.einsum("erd,edf->erf", received, w_gate, preferred_element_type=jnp.float32)
    up_pre = jnp.einsum("erd,edf->erf", received, w_up, preferred_element_type=jnp.float32)
    hidden_f, act_pull = jax.vjp(silu_product, gate_pre, up_pre)
    hidden = hidden_f.astype(jnp.bfloat16)
    expert_out = jnp.einsum(
        "erf,efd->erd", hidden, w_down, preferred_element_type=jnp.float32
    ).astype(jnp.bfloat16)
    returned = lax.all_to_all(
        expert_out, "expert", split_axis=1, concat_axis=0, tiled=True
    ).reshape(n_routed * CAP, model_dim)
    route_out = jnp.einsum(
        "kts,sd->ktd", route_picks, returned, preferred_element_type=jnp.float32
    )
    mixture = jnp.sum(gate_probs.T[:, :, None] * route_out, axis=0)
    output = (residual + mixture).astype(jnp.bfloat16)[None]
    grad_rows = grad_out[0].astype(jnp.float32)
    d_gates = jnp.sum(grad_rows[None] * route_out, axis=-1).T
    d_picked = gate_probs * (d_gates - jnp.sum(gate_probs * d_gates, axis=1, keepdims=True))
    d_logits = jnp.sum(onehot * d_picked[:, :, None], axis=1).astype(jnp.bfloat16)
    d_hidden = jnp.einsum("erd,efd->erf", d_recv, w_down, preferred_element_type=jnp.float32)
    grad_down = expert_term(d_recv, hidden)
    d_gate_f, d_up_f = act_pull(d_hidden)
    d_gate = d_gate_f.astype(jnp.bfloat16)
    d_up = d_up_f.astype(jnp.bfloat16)
    grad_gate = expert_term(received, d_gate)
    grad_upper = expert_term(received, d_up)
    d_in = (
        jnp.einsum("erf,edf->erd", d_gate, w_gate, preferred_element_type=jnp.float32)
        + jnp.einsum("erf,edf->erd", d_up, w_up, preferred_element_type=jnp.float32)
    ).astype(jnp.bfloat16)
    d_back = lax.all_to_all(d_in, "expert", split_axis=1, concat_axis=0, tiled=True).reshape(
        n_routed * CAP, model_dim
    )
    d_normed2 = jnp.dot(token_picks, d_back, preferred_element_type=jnp.float32)
    d_normed2 = d_normed2 + jnp.einsum(
        "te,de->td", d_logits, full_router, preferred_element_type=jnp.float32
    )
    d_resid_norm, grad_gain_two = norm2_pull(d_normed2)
    d_resid = grad_rows + d_resid_norm
    sum_down = lax.psum_scatter(grad_down, "outer", scatter_dimension=1, tiled=True)
    d_branch, sum_down = lax.optimization_barrier((d_resid.astype(jnp.bfloat16), sum_down))
    all_branch = lax.all_gather(d_branch, DP, axis=0, tiled=True)
    gate_low, all_branch = lax.optimization_barrier((grad_gate, all_branch))
    sum_gate = lax.psum_scatter(gate_low, "outer", scatter_dimension=1, tiled=True)
    d_attn = jnp.einsum(
        "td,cd->tc", all_branch, own_out, preferred_element_type=jnp.float32
    ).astype(jnp.bfloat16)
    d_attn_heads = d_attn.reshape(seq_rows, own_heads, head_dim)
    delta = jnp.sum(d_attn_heads.transpose(1, 0, 2).astype(jnp.float32) * attn_heads, axis=-1)
    probs = raw_weights() * inverse_sum[..., None]
    d_probs = jnp.einsum(
        "tgd,sd->gts", d_attn_heads, value_low, preferred_element_type=jnp.float32
    )
    d_score = (probs * (d_probs - delta[..., None])).astype(jnp.bfloat16)
    d_query = score_scale * jnp.einsum(
        "gts,sd->tgd", d_score, key_low, preferred_element_type=jnp.float32
    )
    d_keys = score_scale * jnp.einsum(
        "gts,tgd->sd", d_score, q_low, preferred_element_type=jnp.float32
    )
    d_values = jnp.einsum(
        "gts,tgd->sd", probs.astype(jnp.bfloat16), d_attn_heads, preferred_element_type=jnp.float32
    )
    d_q_f, grad_gain_query = query_pull(d_query)
    d_k_f, grad_gain_key = key_pull(d_keys[:, None, :])
    d_qkv = jnp.concatenate([d_q_f, d_k_f, d_values], axis=1).astype(jnp.bfloat16)
    out_term = jnp.einsum("tc,td->cd", attn_low, all_branch, preferred_element_type=jnp.float32)
    out_term = lax.all_to_all(
        out_term.astype(jnp.bfloat16).reshape((n_expert,) + w_out.shape),
        "expert",
        split_axis=0,
        concat_axis=0,
        tiled=True,
    )
    normed1_term = jnp.einsum("tc,dc->td", d_qkv, own_weights, preferred_element_type=jnp.float32)
    grad_gain_one = (
        jnp.sum(normed1_term * first_normed.astype(jnp.float32), axis=0) / gain_one
    )
    gain_terms = (grad_gain_one, grad_gain_query, grad_gain_key, grad_gain_two)
    normed1_low, sum_gate, out_term, d_qkv, gain_terms = lax.optimization_barrier(
        (pair_sum(normed1_term, 0), sum_gate, out_term, d_qkv, gain_terms)
    )
    d_normed1 = lax.psum_scatter(normed1_low, "outer", scatter_dimension=0, tiled=True)
    qkv_term = jnp.einsum("td,tc->dc", first_normed, d_qkv, preferred_element_type=jnp.float32)
    router_term = jnp.einsum("td,te->de", normed2, d_logits, preferred_element_type=jnp.float32)
    router_term = jnp.pad(router_term, ((0, 0), (0, head_dim - n_routed)))
    grad_blocks = (
        jnp.concatenate([qkv_term, router_term], axis=1)
        .astype(jnp.bfloat16)
        .reshape(n_dp, n_expert, w_rows, -1)
        .transpose(1, 0, 2, 3)
    )
    grad_blocks, gain_terms = lax.optimization_barrier((grad_blocks, gain_terms))
    grad_blocks = lax.all_to_all(grad_blocks, "expert", split_axis=0, concat_axis=0, tiled=True)
    gain_sums = lax.psum(gain_terms, (*DP, "expert"))
    upper_low, d_normed1, grad_blocks, gain_sums = lax.optimization_barrier(
        (grad_upper, d_normed1, grad_blocks, gain_sums)
    )
    sum_upper = lax.psum_scatter(upper_low, "outer", scatter_dimension=1, tiled=True)
    d_tok_norm = norm1_pull(d_normed1.astype(jnp.float32))[0]
    grad_input = (d_resid + d_tok_norm)[None]
    sum_one, sum_query, sum_key, sum_two = gain_sums
    sum_gate = sum_gate.astype(jnp.float32)
    sum_upper = sum_upper.astype(jnp.float32)
    sum_down = sum_down.astype(jnp.float32).transpose(0, 2, 1)
    grad_blocks = jnp.sum(grad_blocks.astype(jnp.float32), axis=0).astype(jnp.bfloat16)
    grad_blocks = lax.all_to_all(
        grad_blocks, DP, split_axis=0, concat_axis=0, tiled=True
    ).astype(jnp.float32)

    def gather_heads(first):
        picked = grad_blocks[:, :, first : first + head_dim]
        picked = jnp.sum(picked.reshape(heads_kv, share, w_rows, head_dim), axis=1)
        return picked.transpose(1, 0, 2).reshape(w_rows, heads_kv * head_dim)

    sum_wq = grad_blocks[:, :, :q_cols].transpose(1, 0, 2).reshape(w_rows, heads_q * head_dim)
    sum_wk = gather_heads(q_cols)
    sum_wv = gather_heads(q_cols + head_dim)
    sum_wr = jnp.sum(grad_blocks[:, :, qkv_cols : qkv_cols + n_routed], axis=0)
    sum_wo = jnp.sum(out_term.astype(jnp.float32), axis=0)
    return (
        output,
        grad_input,
        sum_one,
        sum_wq,
        sum_wk,
        sum_wv,
        sum_query,
        sum_key,
        sum_wo,
        sum_two,
        sum_wr,
        sum_gate,
        sum_upper,
        sum_down,
    )


def solution(mesh):
    n_dp, n_expert = mesh.devices.shape
    view = jax.sharding.Mesh(
        mesh.devices.reshape(n_dp // 2, 2, n_expert), ("outer", "core", "expert")
    )
    rows = P((*DP, "expert"), None)
    return jax.shard_map(
        shards,
        mesh=view,
        in_specs=(
            P("expert", DP, None),
            P(),
            rows,
            rows,
            rows,
            P(),
            P(),
            rows,
            P(),
            rows,
            P("expert", None, None),
            P("expert", None, None),
            P("expert", None, None),
            P("expert", DP),
            P("expert", DP, None),
            P("expert", DP, None),
        ),
        out_specs=(
            P("expert", DP, None),
            P("expert", DP, None),
            P(),
            rows,
            rows,
            rows,
            P(),
            P(),
            rows,
            P(),
            rows,
            P("expert", DP, None),
            P("expert", DP, None),
            P("expert", None, DP),
        ),
        check_vma=False,
    )
```

```python
import jax
import jax.numpy as jnp
from jax import lax
from jax.sharding import PartitionSpec as P

CAP = 48
DP = ("outer", "core")


EPSILON = 1e-06
THETA_BASE = 1000000.0
MASKED = -1e30


def norm_rows(values, gain):
    return values * lax.rsqrt(jnp.mean(values * values, axis=-1, keepdims=True) + EPSILON) * gain


def rotate_half(values):
    middle = values.shape[-1] // 2
    return jnp.concatenate([-values[..., middle:], values[..., :middle]], axis=-1)


def rope_tables(positions, head_width):
    freq_index = jnp.arange(head_width // 2).astype(jnp.float32)
    inverse = THETA_BASE ** (-2.0 * freq_index / head_width)
    angles = positions.astype(jnp.float32)[:, None] * inverse[None, :]
    angles = jnp.concatenate([angles, angles], axis=-1)
    return (jnp.cos(angles)[:, None, :], jnp.sin(angles)[:, None, :])


def prepare_heads(raw, gain, cosine_table, sine_table, heads):
    normed = norm_rows(raw.reshape(raw.shape[0], heads, -1), gain)
    return normed * cosine_table + rotate_half(normed) * sine_table


def silu_product(gate_pre, up_pre):
    return jax.nn.silu(gate_pre) * up_pre


def pair_sum(values, axis):
    values = values.astype(jnp.bfloat16)
    size = values.shape[axis] // lax.axis_size(DP)
    split = values.shape[:axis] + (-1, 2, size) + values.shape[axis + 1 :]
    merged = values.shape[:axis] + (-1,) + values.shape[axis + 1 :]
    core = lax.axis_index("core")

    def pick(index):
        return lax.dynamic_index_in_dim(values.reshape(split), index, axis + 1, keepdims=False)

    arrived = lax.ppermute(pick(1 - core), "core", [(0, 1), (1, 0)])
    total = pick(core).astype(jnp.float32) + arrived.astype(jnp.float32)
    return total.astype(jnp.bfloat16).reshape(merged)


def expert_term(rows, weights):
    return pair_sum(
        jnp.einsum("erd,erf->edf", rows, weights, preferred_element_type=jnp.float32), 1
    )


def slot_table(chosen, n_routed):
    rows, top_count = chosen.shape[-2:]
    flat = chosen.reshape(-1, rows * top_count)
    onehot = (flat[:, :, None] == jnp.arange(n_routed, dtype=jnp.int32)).astype(jnp.float32)
    index = jnp.arange(rows * top_count, dtype=jnp.int32)
    earlier = (index[:, None] > index[None, :]).astype(jnp.bfloat16)
    counts = jnp.einsum(
        "ij,sje->sie", earlier, onehot.astype(jnp.bfloat16), preferred_element_type=jnp.float32
    )
    ranks = jnp.sum(counts * onehot, axis=2).astype(jnp.int32)
    return (flat * CAP + ranks).reshape(chosen.shape)


def choose_gates(normed, router, chosen):
    logits = jnp.dot(normed, router, preferred_element_type=jnp.float32)
    experts = jnp.arange(router.shape[1], dtype=jnp.int32)
    onehot = (chosen[:, :, None] == experts).astype(jnp.float32)
    return (jax.nn.softmax(jnp.sum(onehot * logits[:, None, :], axis=2), axis=-1), onehot)


def shards(
    tokens,
    norm1,
    w_query,
    key_projection,
    value_projection,
    q_gain,
    key_norm_gain,
    w_out,
    norm2,
    w_router,
    w_gate,
    w_up,
    w_down,
    segments,
    routes,
    grad_out,
):
    tok_in = tokens[0].astype(jnp.float32)
    tok_rows, model_dim = tok_in.shape
    head_dim = q_gain.shape[0]
    heads_q = w_query.shape[1] // head_dim
    heads_kv = key_projection.shape[1] // head_dim
    n_dp = lax.axis_size(DP)
    n_expert = lax.axis_size("expert")
    w_rows = w_query.shape[0]
    own_heads = heads_q // n_dp
    share = n_dp // heads_kv
    q_cols = own_heads * head_dim
    n_routed = w_router.shape[1]
    top_count = routes.shape[2]
    score_scale = head_dim ** (-0.5)
    gain_one = norm1.astype(jnp.float32)
    gain_two = norm2.astype(jnp.float32)
    gain_query = q_gain.astype(jnp.float32)
    gain_key = key_norm_gain.astype(jnp.float32)
    normed1_f, norm1_pull = jax.vjp(norm_rows, tok_in, gain_one)
    segment = lax.all_gather(segments[0].astype(jnp.bfloat16), DP, axis=0, tiled=True)
    seq_rows = segment.shape[0]

    def spread_heads(matrix):
        return jnp.repeat(matrix.reshape(w_rows, heads_kv, head_dim), share, axis=1)

    router_pad = jnp.pad(w_router, ((0, 0), (0, head_dim - n_routed)))
    blocks = jnp.concatenate(
        [
            w_query.reshape(w_rows, n_dp, q_cols),
            spread_heads(key_projection),
            spread_heads(value_projection),
            jnp.broadcast_to(router_pad[:, None, :], (w_rows, n_dp, head_dim)),
        ],
        axis=2,
    ).transpose(1, 0, 2)
    blocks = lax.all_to_all(blocks, DP, split_axis=0, concat_axis=0, tiled=True)

    def spread_expert(piece):
        copies = jnp.broadcast_to(piece[None], (n_expert,) + piece.shape)
        return lax.all_to_all(copies, "expert", split_axis=0, concat_axis=0, tiled=True)

    def expert_major(values):
        split = values.reshape(values.shape[0], n_dp, n_expert, w_rows)
        return split.transpose(0, 2, 1, 3).reshape(values.shape[0], model_dim)

    def row_major(values):
        split = values.reshape(values.shape[0], n_expert, n_dp, w_rows)
        return split.transpose(0, 2, 1, 3).reshape(values.shape[0], model_dim)

    first_normed = expert_major(normed1_f.astype(jnp.bfloat16))
    first_normed, blocks = lax.optimization_barrier((first_normed, blocks))
    first_normed = lax.all_gather(first_normed, DP, axis=0, tiled=True)
    all_routes = lax.all_gather(routes[0], "expert", axis=0)
    blocks, w_out, all_routes, segment = lax.optimization_barrier(
        (spread_expert(blocks), w_out, all_routes, segment)
    )
    own_weights = blocks.reshape(model_dim, -1)
    qkv_cols = q_cols + 2 * head_dim
    full_router = row_major(own_weights[:, qkv_cols : qkv_cols + n_routed].T).T
    own_weights = own_weights[:, :qkv_cols]
    own_out = spread_expert(w_out).reshape(q_cols, model_dim)
    raw = jnp.dot(first_normed, own_weights, preferred_element_type=jnp.float32)
    q_raw = raw[:, :q_cols]
    key_unrotated = raw[:, q_cols : q_cols + head_dim]
    value_low = raw[:, q_cols + head_dim :].astype(jnp.bfloat16)
    positions = jnp.arange(seq_rows, dtype=jnp.int32)
    cosine_table, sine_table = rope_tables(positions, head_dim)
    q_rot, query_pull = jax.vjp(
        lambda raw_in, gain_in: prepare_heads(raw_in, gain_in, cosine_table, sine_table, own_heads),
        q_raw,
        gain_query,
    )
    k_rot, key_pull = jax.vjp(
        lambda raw_in, gain_in: prepare_heads(raw_in, gain_in, cosine_table, sine_table, 1),
        key_unrotated,
        gain_key,
    )
    q_low = q_rot.astype(jnp.bfloat16)
    key_low = k_rot.astype(jnp.bfloat16).reshape(seq_rows, head_dim)
    allowed = (
        (positions[:, None] >= positions[None, :]) & (segment[:, None] == segment[None, :])
    )[None]

    def raw_weights():
        score = jnp.einsum("tgd,sd->gts", q_low, key_low, preferred_element_type=jnp.float32)
        return jnp.where(allowed, jnp.exp(score * score_scale), 0.0)

    weights = raw_weights()
    inverse_sum = 1.0 / jnp.sum(weights, axis=-1)
    attn_heads = (
        jnp.einsum(
            "gts,sd->gtd", weights.astype(jnp.bfloat16), value_low, preferred_element_type=jnp.float32
        )
        * inverse_sum[..., None]
    )
    attn_low = attn_heads.transpose(1, 0, 2).reshape(seq_rows, q_cols).astype(jnp.bfloat16)
    branch_term = jnp.dot(attn_low, own_out, preferred_element_type=jnp.float32)
    branch_low, late_grad = lax.optimization_barrier((branch_term.astype(jnp.bfloat16), grad_out[0]))
    branch = lax.psum_scatter(branch_low, DP, scatter_dimension=0, tiled=True)
    branch, all_grad = lax.optimization_barrier((branch, spread_expert(late_grad)))
    residual = tok_in + branch.astype(jnp.float32)
    normed2_f, norm2_pull = jax.vjp(norm_rows, residual, gain_two)
    normed2 = normed2_f.astype(jnp.bfloat16)
    all_normed = spread_expert(normed2)
    chosen = routes[0]
    gate_probs, onehot = choose_gates(normed2, full_router, chosen)
    slot_count = n_routed * CAP
    slots = slot_table(chosen, n_routed)
    slot_hits = slots[:, :, None] == jnp.arange(slot_count, dtype=jnp.int32)
    route_picks = slot_hits.astype(jnp.bfloat16).transpose(1, 0, 2)
    token_picks = jnp.any(slot_hits, axis=1).astype(jnp.bfloat16)
    held = w_gate.shape[0]
    first_slot = lax.axis_index("expert") * (held * CAP)
    all_hits = (slot_table(all_routes, n_routed) - first_slot)[..., None] == jnp.arange(
        held * CAP, dtype=jnp.int32
    )
    all_picks = jnp.any(all_hits, axis=2).astype(jnp.bfloat16)

    def to_slots(rows):
        return jnp.einsum("stl,std->sld", all_picks, rows, preferred_element_type=jnp.float32)

    def by_expert(rows):
        rows = rows.reshape(n_expert, held, CAP, model_dim).transpose(1, 0, 2, 3)
        return rows.reshape(held, n_expert * CAP, model_dim)

    all_gates, _ = choose_gates(
        all_normed.reshape(-1, model_dim), full_router, all_routes.reshape(-1, top_count)
    )
    all_gates = all_gates.reshape(all_routes.shape)
    slot_gate = jnp.sum(jnp.where(all_hits, all_gates[..., None], 0.0), axis=(1, 2))
    received = by_expert(to_slots(all_normed).astype(jnp.bfloat16))
    d_recv = by_expert((slot_gate[:, :, None] * to_slots(all_grad)).astype(jnp.bfloat16))
    gate_pre = jnp.einsum("erd,edf->erf", received, w_gate, preferred_element_type=jnp.float32)
    up_pre = jnp.einsum("erd,edf->erf", received, w_up, preferred_element_type=jnp.float32)
    hidden_f, act_pull = jax.vjp(silu_product, gate_pre, up_pre)
    hidden = hidden_f.astype(jnp.bfloat16)
    expert_out = jnp.einsum(
        "erf,efd->erd", hidden, w_down, preferred_element_type=jnp.float32
    ).astype(jnp.bfloat16)
    returned = lax.all_to_all(
        expert_out, "expert", split_axis=1, concat_axis=0, tiled=True
    ).reshape(n_routed * CAP, model_dim)
    route_out = jnp.einsum(
        "kts,sd->ktd", route_picks, returned, preferred_element_type=jnp.float32
    )
    mixture = jnp.sum(gate_probs.T[:, :, None] * route_out, axis=0)
    output = (residual + mixture).astype(jnp.bfloat16)[None]
    grad_rows = grad_out[0].astype(jnp.float32)
    d_gates = jnp.sum(grad_rows[None] * route_out, axis=-1).T
    d_picked = gate_probs * (d_gates - jnp.sum(gate_probs * d_gates, axis=1, keepdims=True))
    d_logits = jnp.sum(onehot * d_picked[:, :, None], axis=1).astype(jnp.bfloat16)
    d_hidden = jnp.einsum("erd,efd->erf", d_recv, w_down, preferred_element_type=jnp.float32)
    grad_down = jnp.einsum(
        "erd,erf->edf", d_recv, hidden, preferred_element_type=jnp.float32
    ).astype(jnp.bfloat16)
    d_gate_f, d_up_f = act_pull(d_hidden)
    d_gate = d_gate_f.astype(jnp.bfloat16)
    d_up = d_up_f.astype(jnp.bfloat16)
    grad_gate = expert_term(received, d_gate)
    grad_upper = expert_term(received, d_up)
    d_in = (
        jnp.einsum("erf,edf->erd", d_gate, w_gate, preferred_element_type=jnp.float32)
        + jnp.einsum("erf,edf->erd", d_up, w_up, preferred_element_type=jnp.float32)
    ).astype(jnp.bfloat16)
    d_back = lax.all_to_all(d_in, "expert", split_axis=1, concat_axis=0, tiled=True).reshape(
        n_routed * CAP, model_dim
    )
    d_normed2 = jnp.dot(token_picks, d_back, preferred_element_type=jnp.float32)
    d_normed2 = d_normed2 + jnp.einsum(
        "te,de->td", d_logits, full_router, preferred_element_type=jnp.float32
    )
    d_resid_norm, grad_gain_two = norm2_pull(d_normed2)
    d_resid = grad_rows + d_resid_norm
    sum_down = lax.psum_scatter(grad_down, DP, scatter_dimension=1, tiled=True)
    d_branch, sum_down = lax.optimization_barrier((d_resid.astype(jnp.bfloat16), sum_down))
    all_branch = lax.all_gather(d_branch, DP, axis=0, tiled=True)
    gate_low, all_branch = lax.optimization_barrier((grad_gate, all_branch))
    sum_gate = lax.psum_scatter(gate_low, "outer", scatter_dimension=1, tiled=True)
    d_attn = jnp.einsum(
        "td,cd->tc", all_branch, own_out, preferred_element_type=jnp.float32
    ).astype(jnp.bfloat16)
    d_attn_heads = d_attn.reshape(seq_rows, own_heads, head_dim)
    delta = jnp.sum(d_attn_heads.transpose(1, 0, 2).astype(jnp.float32) * attn_heads, axis=-1)
    probs = raw_weights() * inverse_sum[..., None]
    d_probs = jnp.einsum(
        "tgd,sd->gts", d_attn_heads, value_low, preferred_element_type=jnp.float32
    )
    d_score = (probs * (d_probs - delta[..., None])).astype(jnp.bfloat16)
    d_query = score_scale * jnp.einsum(
        "gts,sd->tgd", d_score, key_low, preferred_element_type=jnp.float32
    )
    d_keys = score_scale * jnp.einsum(
        "gts,tgd->sd", d_score, q_low, preferred_element_type=jnp.float32
    )
    d_values = jnp.einsum(
        "gts,tgd->sd", probs.astype(jnp.bfloat16), d_attn_heads, preferred_element_type=jnp.float32
    )
    d_q_f, grad_gain_query = query_pull(d_query)
    d_k_f, grad_gain_key = key_pull(d_keys[:, None, :])
    d_qkv = jnp.concatenate([d_q_f, d_k_f, d_values], axis=1).astype(jnp.bfloat16)
    out_term = jnp.einsum("tc,td->cd", attn_low, all_branch, preferred_element_type=jnp.float32)
    out_term = lax.all_to_all(
        out_term.astype(jnp.bfloat16).reshape((n_expert,) + w_out.shape),
        "expert",
        split_axis=0,
        concat_axis=0,
        tiled=True,
    )
    normed1_term = jnp.einsum("tc,dc->td", d_qkv, own_weights, preferred_element_type=jnp.float32)
    grad_gain_one = (
        row_major(jnp.sum(normed1_term * first_normed.astype(jnp.float32), axis=0)[None])[0]
        / gain_one
    )
    gain_terms = (grad_gain_one, grad_gain_query, grad_gain_key, grad_gain_two)
    normed1_low, sum_gate, out_term, d_qkv, gain_terms = lax.optimization_barrier(
        (pair_sum(normed1_term, 0), sum_gate, out_term, d_qkv, gain_terms)
    )
    d_normed1 = lax.psum_scatter(normed1_low, "outer", scatter_dimension=0, tiled=True)
    qkv_term = jnp.einsum("td,tc->dc", first_normed, d_qkv, preferred_element_type=jnp.float32)
    router_term = jnp.einsum("te,td->ed", d_logits, normed2, preferred_element_type=jnp.float32)
    router_term = expert_major(router_term).T
    gain_cols = -(-sum(term.shape[0] for term in gain_terms) // w_rows)
    flat_gains = jnp.concatenate(gain_terms)
    flat_gains = jnp.pad(flat_gains, (0, gain_cols * w_rows - flat_gains.shape[0]))
    gain_block = jnp.broadcast_to(
        flat_gains.reshape(w_rows, gain_cols)[None], (n_dp * n_expert, w_rows, gain_cols)
    ).reshape(model_dim, gain_cols)
    tail_cols = -(-(n_routed + gain_cols) // head_dim) * head_dim
    spare = jnp.zeros((model_dim, tail_cols - n_routed - gain_cols), jnp.float32)
    grad_blocks = (
        jnp.concatenate([qkv_term, router_term, gain_block, spare], axis=1)
        .astype(jnp.bfloat16)
        .reshape(n_expert, n_dp, w_rows, -1)
    )
    grad_blocks = lax.all_to_all(grad_blocks, "expert", split_axis=0, concat_axis=0, tiled=True)
    upper_low, d_normed1, grad_blocks = lax.optimization_barrier(
        (grad_upper, d_normed1, grad_blocks)
    )
    sum_upper = lax.psum_scatter(upper_low, "outer", scatter_dimension=1, tiled=True)
    d_tok_norm = norm1_pull(row_major(d_normed1).astype(jnp.float32))[0]
    grad_input = (d_resid + d_tok_norm)[None]
    sum_gate = sum_gate.astype(jnp.float32)
    sum_upper = sum_upper.astype(jnp.float32)
    sum_down = sum_down.astype(jnp.float32).transpose(0, 2, 1)
    grad_blocks = jnp.sum(grad_blocks.astype(jnp.float32), axis=0).astype(jnp.bfloat16)
    grad_blocks = lax.all_to_all(
        grad_blocks, DP, split_axis=0, concat_axis=0, tiled=True
    ).astype(jnp.float32)

    def gather_heads(first):
        picked = grad_blocks[:, :, first : first + head_dim]
        picked = jnp.sum(picked.reshape(heads_kv, share, w_rows, head_dim), axis=1)
        return picked.transpose(1, 0, 2).reshape(w_rows, heads_kv * head_dim)

    sum_wq = grad_blocks[:, :, :q_cols].transpose(1, 0, 2).reshape(w_rows, heads_q * head_dim)
    sum_wk = gather_heads(q_cols)
    sum_wv = gather_heads(q_cols + head_dim)
    tail_sum = jnp.sum(grad_blocks[:, :, qkv_cols:], axis=0)
    sum_wr = tail_sum[:, :n_routed]
    flat_gains = tail_sum[:, n_routed : n_routed + gain_cols].reshape(-1)
    ends = (model_dim, model_dim + head_dim, model_dim + 2 * head_dim, 2 * model_dim + 2 * head_dim)
    sum_one = flat_gains[: ends[0]]
    sum_query = flat_gains[ends[0] : ends[1]]
    sum_key = flat_gains[ends[1] : ends[2]]
    sum_two = flat_gains[ends[2] : ends[3]]
    sum_wo = jnp.sum(out_term.astype(jnp.float32), axis=0)
    return (
        output,
        grad_input,
        sum_one,
        sum_wq,
        sum_wk,
        sum_wv,
        sum_query,
        sum_key,
        sum_wo,
        sum_two,
        sum_wr,
        sum_gate,
        sum_upper,
        sum_down,
    )


def solution(mesh):
    n_dp, n_expert = mesh.devices.shape
    view = jax.sharding.Mesh(
        mesh.devices.reshape(n_dp // 2, 2, n_expert), ("outer", "core", "expert")
    )
    rows = P((*DP, "expert"), None)
    return jax.shard_map(
        shards,
        mesh=view,
        in_specs=(
            P("expert", DP, None),
            P(),
            rows,
            rows,
            rows,
            P(),
            P(),
            rows,
            P(),
            rows,
            P("expert", None, None),
            P("expert", None, None),
            P("expert", None, None),
            P("expert", DP),
            P("expert", DP, None),
            P("expert", DP, None),
        ),
        out_specs=(
            P("expert", DP, None),
            P("expert", DP, None),
            P(),
            rows,
            rows,
            rows,
            P(),
            P(),
            rows,
            P(),
            rows,
            P("expert", DP, None),
            P("expert", DP, None),
            P("expert", None, DP),
        ),
        check_vma=False,
    )
```

```python
import jax
import jax.numpy as jnp
from jax import lax
from jax.sharding import PartitionSpec as P

CAP = 48
DP = ("outer", "core")


EPSILON = 1e-06
THETA_BASE = 1000000.0
MASKED = -1e30


def norm_rows(values, gain):
    return values * lax.rsqrt(jnp.mean(values * values, axis=-1, keepdims=True) + EPSILON) * gain


def rotate_half(values):
    middle = values.shape[-1] // 2
    return jnp.concatenate([-values[..., middle:], values[..., :middle]], axis=-1)


def rope_tables(positions, head_width):
    freq_index = jnp.arange(head_width // 2).astype(jnp.float32)
    inverse = THETA_BASE ** (-2.0 * freq_index / head_width)
    angles = positions.astype(jnp.float32)[:, None] * inverse[None, :]
    angles = jnp.concatenate([angles, angles], axis=-1)
    return (jnp.cos(angles)[:, None, :], jnp.sin(angles)[:, None, :])


def prepare_heads(raw, gain, cosine_table, sine_table, heads):
    normed = norm_rows(raw.reshape(raw.shape[0], heads, -1), gain)
    return normed * cosine_table + rotate_half(normed) * sine_table


def silu_product(gate_pre, up_pre):
    return jax.nn.silu(gate_pre) * up_pre


def pair_sum(values, axis):
    values = values.astype(jnp.bfloat16)
    size = values.shape[axis] // lax.axis_size(DP)
    split = values.shape[:axis] + (-1, 2, size) + values.shape[axis + 1 :]
    merged = values.shape[:axis] + (-1,) + values.shape[axis + 1 :]
    core = lax.axis_index("core")

    def pick(index):
        return lax.dynamic_index_in_dim(values.reshape(split), index, axis + 1, keepdims=False)

    arrived = lax.ppermute(pick(1 - core), "core", [(0, 1), (1, 0)])
    total = pick(core).astype(jnp.float32) + arrived.astype(jnp.float32)
    return total.astype(jnp.bfloat16).reshape(merged)


def expert_term(rows, weights):
    return pair_sum(
        jnp.einsum("erd,erf->edf", rows, weights, preferred_element_type=jnp.float32), 1
    )


def slot_table(chosen, n_routed):
    rows, top_count = chosen.shape[-2:]
    flat = chosen.reshape(-1, rows * top_count)
    onehot = (flat[:, :, None] == jnp.arange(n_routed, dtype=jnp.int32)).astype(jnp.float32)
    index = jnp.arange(rows * top_count, dtype=jnp.int32)
    earlier = (index[:, None] > index[None, :]).astype(jnp.bfloat16)
    counts = jnp.einsum(
        "ij,sje->sie", earlier, onehot.astype(jnp.bfloat16), preferred_element_type=jnp.float32
    )
    ranks = jnp.sum(counts * onehot, axis=2).astype(jnp.int32)
    return (flat * CAP + ranks).reshape(chosen.shape)


def choose_gates(normed, router, chosen):
    logits = jnp.dot(normed, router, preferred_element_type=jnp.float32)
    experts = jnp.arange(router.shape[1], dtype=jnp.int32)
    onehot = (chosen[:, :, None] == experts).astype(jnp.float32)
    return (jax.nn.softmax(jnp.sum(onehot * logits[:, None, :], axis=2), axis=-1), onehot)


def shards(
    tokens,
    norm1,
    w_query,
    key_projection,
    value_projection,
    q_gain,
    key_norm_gain,
    w_out,
    norm2,
    w_router,
    w_gate,
    w_up,
    w_down,
    segments,
    routes,
    grad_out,
):
    tok_in = tokens[0].astype(jnp.float32)
    tok_rows, model_dim = tok_in.shape
    head_dim = q_gain.shape[0]
    heads_q = w_query.shape[1] // head_dim
    heads_kv = key_projection.shape[1] // head_dim
    n_dp = lax.axis_size(DP)
    n_expert = lax.axis_size("expert")
    w_rows = w_query.shape[0]
    own_heads = heads_q // n_dp
    share = n_dp // heads_kv
    q_cols = own_heads * head_dim
    n_routed = w_router.shape[1]
    top_count = routes.shape[2]
    score_scale = head_dim ** (-0.5)
    gain_one = norm1.astype(jnp.float32)
    gain_two = norm2.astype(jnp.float32)
    gain_query = q_gain.astype(jnp.float32)
    gain_key = key_norm_gain.astype(jnp.float32)
    normed1_f, norm1_pull = jax.vjp(norm_rows, tok_in, gain_one)
    segment = lax.all_gather(segments[0].astype(jnp.bfloat16), DP, axis=0, tiled=True)
    seq_rows = segment.shape[0]

    def spread_heads(matrix):
        return jnp.repeat(matrix.reshape(w_rows, heads_kv, head_dim), share, axis=1)

    router_pad = jnp.pad(w_router, ((0, 0), (0, head_dim - n_routed)))
    blocks = jnp.concatenate(
        [
            w_query.reshape(w_rows, n_dp, q_cols),
            spread_heads(key_projection),
            spread_heads(value_projection),
            jnp.broadcast_to(router_pad[:, None, :], (w_rows, n_dp, head_dim)),
        ],
        axis=2,
    ).transpose(1, 0, 2)
    blocks = lax.all_to_all(blocks, DP, split_axis=0, concat_axis=0, tiled=True)

    def spread_expert(piece):
        copies = jnp.broadcast_to(piece[None], (n_expert,) + piece.shape)
        return lax.all_to_all(copies, "expert", split_axis=0, concat_axis=0, tiled=True)

    def expert_major(values):
        split = values.reshape(values.shape[0], n_dp, n_expert, w_rows)
        return split.transpose(0, 2, 1, 3).reshape(values.shape[0], model_dim)

    def row_major(values):
        split = values.reshape(values.shape[0], n_expert, n_dp, w_rows)
        return split.transpose(0, 2, 1, 3).reshape(values.shape[0], model_dim)

    first_normed = expert_major(normed1_f.astype(jnp.bfloat16))
    first_normed, blocks = lax.optimization_barrier((first_normed, blocks))
    first_normed = lax.all_gather(first_normed, DP, axis=0, tiled=True)
    all_routes = lax.all_gather(routes[0], "expert", axis=0)
    blocks, w_out, all_routes, segment = lax.optimization_barrier(
        (spread_expert(blocks), w_out, all_routes, segment)
    )
    own_weights = blocks.reshape(model_dim, -1)
    qkv_cols = q_cols + 2 * head_dim
    full_router = row_major(own_weights[:, qkv_cols : qkv_cols + n_routed].T).T
    own_weights = own_weights[:, :qkv_cols]
    own_out = spread_expert(w_out).reshape(q_cols, model_dim)
    raw = jnp.dot(first_normed, own_weights, preferred_element_type=jnp.float32)
    q_raw = raw[:, :q_cols]
    key_unrotated = raw[:, q_cols : q_cols + head_dim]
    value_low = raw[:, q_cols + head_dim :].astype(jnp.bfloat16)
    positions = jnp.arange(seq_rows, dtype=jnp.int32)
    cosine_table, sine_table = rope_tables(positions, head_dim)
    q_rot, query_pull = jax.vjp(
        lambda raw_in, gain_in: prepare_heads(raw_in, gain_in, cosine_table, sine_table, own_heads),
        q_raw,
        gain_query,
    )
    k_rot, key_pull = jax.vjp(
        lambda raw_in, gain_in: prepare_heads(raw_in, gain_in, cosine_table, sine_table, 1),
        key_unrotated,
        gain_key,
    )
    q_low = q_rot.astype(jnp.bfloat16)
    key_low = k_rot.astype(jnp.bfloat16).reshape(seq_rows, head_dim)
    allowed = (
        (positions[:, None] >= positions[None, :]) & (segment[:, None] == segment[None, :])
    )[None]

    def raw_weights():
        score = jnp.einsum("tgd,sd->gts", q_low, key_low, preferred_element_type=jnp.float32)
        return jnp.where(allowed, jnp.exp(score * score_scale), 0.0)

    weights = raw_weights()
    inverse_sum = 1.0 / jnp.sum(weights, axis=-1)
    attn_heads = (
        jnp.einsum(
            "gts,sd->gtd", weights.astype(jnp.bfloat16), value_low, preferred_element_type=jnp.float32
        )
        * inverse_sum[..., None]
    )
    attn_low = attn_heads.transpose(1, 0, 2).reshape(seq_rows, q_cols).astype(jnp.bfloat16)
    branch_term = jnp.dot(attn_low, own_out, preferred_element_type=jnp.float32)
    branch_low, late_grad = lax.optimization_barrier((branch_term.astype(jnp.bfloat16), grad_out[0]))
    branch = lax.psum_scatter(branch_low, DP, scatter_dimension=0, tiled=True)
    branch, all_grad = lax.optimization_barrier((branch, spread_expert(late_grad)))
    residual = tok_in + branch.astype(jnp.float32)
    normed2_f, norm2_pull = jax.vjp(norm_rows, residual, gain_two)
    normed2 = normed2_f.astype(jnp.bfloat16)
    all_normed = spread_expert(normed2)
    chosen = routes[0]
    gate_probs, onehot = choose_gates(normed2, full_router, chosen)
    slot_count = n_routed * CAP
    slots = slot_table(chosen, n_routed)
    slot_hits = slots[:, :, None] == jnp.arange(slot_count, dtype=jnp.int32)
    route_picks = slot_hits.astype(jnp.bfloat16).transpose(1, 0, 2)
    token_picks = jnp.any(slot_hits, axis=1).astype(jnp.bfloat16)
    held = w_gate.shape[0]
    first_slot = lax.axis_index("expert") * (held * CAP)
    all_hits = (slot_table(all_routes, n_routed) - first_slot)[..., None] == jnp.arange(
        held * CAP, dtype=jnp.int32
    )
    all_picks = jnp.any(all_hits, axis=2).astype(jnp.bfloat16)

    def to_slots(rows):
        return jnp.einsum("stl,std->sld", all_picks, rows, preferred_element_type=jnp.float32)

    def by_expert(rows):
        rows = rows.reshape(n_expert, held, CAP, model_dim).transpose(1, 0, 2, 3)
        return rows.reshape(held, n_expert * CAP, model_dim)

    all_gates, _ = choose_gates(
        all_normed.reshape(-1, model_dim), full_router, all_routes.reshape(-1, top_count)
    )
    all_gates = all_gates.reshape(all_routes.shape)
    slot_gate = jnp.sum(jnp.where(all_hits, all_gates[..., None], 0.0), axis=(1, 2))
    received = by_expert(to_slots(all_normed).astype(jnp.bfloat16))
    d_recv = by_expert((slot_gate[:, :, None] * to_slots(all_grad)).astype(jnp.bfloat16))
    gate_pre = jnp.einsum("erd,edf->erf", received, w_gate, preferred_element_type=jnp.float32)
    up_pre = jnp.einsum("erd,edf->erf", received, w_up, preferred_element_type=jnp.float32)
    hidden_f, act_pull = jax.vjp(silu_product, gate_pre, up_pre)
    hidden = hidden_f.astype(jnp.bfloat16)
    expert_out = jnp.einsum(
        "erf,efd->erd", hidden, w_down, preferred_element_type=jnp.float32
    ).astype(jnp.bfloat16)
    returned = lax.all_to_all(
        expert_out, "expert", split_axis=1, concat_axis=0, tiled=True
    ).reshape(n_routed * CAP, model_dim)
    route_out = jnp.einsum(
        "kts,sd->ktd", route_picks, returned, preferred_element_type=jnp.float32
    )
    mixture = jnp.sum(gate_probs.T[:, :, None] * route_out, axis=0)
    output = (residual + mixture).astype(jnp.bfloat16)[None]
    grad_rows = grad_out[0].astype(jnp.float32)
    d_gates = jnp.sum(grad_rows[None] * route_out, axis=-1).T
    d_picked = gate_probs * (d_gates - jnp.sum(gate_probs * d_gates, axis=1, keepdims=True))
    d_logits = jnp.sum(onehot * d_picked[:, :, None], axis=1).astype(jnp.bfloat16)
    d_hidden = jnp.einsum("erd,efd->erf", d_recv, w_down, preferred_element_type=jnp.float32)
    grad_down = jnp.einsum(
        "erd,erf->edf", d_recv, hidden, preferred_element_type=jnp.float32
    ).astype(jnp.bfloat16)
    d_gate_f, d_up_f = act_pull(d_hidden)
    d_gate = d_gate_f.astype(jnp.bfloat16)
    d_up = d_up_f.astype(jnp.bfloat16)
    grad_gate = expert_term(received, d_gate)
    grad_upper = expert_term(received, d_up)
    d_in = (
        jnp.einsum("erf,edf->erd", d_gate, w_gate, preferred_element_type=jnp.float32)
        + jnp.einsum("erf,edf->erd", d_up, w_up, preferred_element_type=jnp.float32)
    ).astype(jnp.bfloat16)
    d_back = lax.all_to_all(d_in, "expert", split_axis=1, concat_axis=0, tiled=True).reshape(
        n_routed * CAP, model_dim
    )
    d_normed2 = jnp.dot(token_picks, d_back, preferred_element_type=jnp.float32)
    d_normed2 = d_normed2 + jnp.einsum(
        "te,de->td", d_logits, full_router, preferred_element_type=jnp.float32
    )
    d_resid_norm, grad_gain_two = norm2_pull(d_normed2)
    d_resid = grad_rows + d_resid_norm
    sum_down = lax.psum_scatter(grad_down, DP, scatter_dimension=1, tiled=True)
    d_branch, sum_down = lax.optimization_barrier((d_resid.astype(jnp.bfloat16), sum_down))
    all_branch = lax.all_gather(d_branch, DP, axis=0, tiled=True)
    gate_low, all_branch = lax.optimization_barrier((grad_gate, all_branch))
    sum_gate = lax.psum_scatter(gate_low, "outer", scatter_dimension=1, tiled=True)
    d_attn = jnp.einsum(
        "td,cd->tc", all_branch, own_out, preferred_element_type=jnp.float32
    ).astype(jnp.bfloat16)
    d_attn_heads = d_attn.reshape(seq_rows, own_heads, head_dim)
    delta = jnp.sum(d_attn_heads.transpose(1, 0, 2).astype(jnp.float32) * attn_heads, axis=-1)
    probs = raw_weights() * inverse_sum[..., None]
    d_probs = jnp.einsum(
        "tgd,sd->gts", d_attn_heads, value_low, preferred_element_type=jnp.float32
    )
    d_score = (probs * (d_probs - delta[..., None])).astype(jnp.bfloat16)
    d_query = score_scale * jnp.einsum(
        "gts,sd->tgd", d_score, key_low, preferred_element_type=jnp.float32
    )
    d_keys = score_scale * jnp.einsum(
        "gts,tgd->sd", d_score, q_low, preferred_element_type=jnp.float32
    )
    d_values = jnp.einsum(
        "gts,tgd->sd", probs.astype(jnp.bfloat16), d_attn_heads, preferred_element_type=jnp.float32
    )
    d_q_f, grad_gain_query = query_pull(d_query)
    d_k_f, grad_gain_key = key_pull(d_keys[:, None, :])
    d_qkv = jnp.concatenate([d_q_f, d_k_f, d_values], axis=1).astype(jnp.bfloat16)
    out_term = jnp.einsum("tc,td->cd", attn_low, all_branch, preferred_element_type=jnp.float32)
    normed1_term = jnp.einsum("tc,dc->td", d_qkv, own_weights, preferred_element_type=jnp.float32)
    grad_gain_one = (
        row_major(jnp.sum(normed1_term * first_normed.astype(jnp.float32), axis=0)[None])[0]
        / gain_one
    )
    gain_terms = (grad_gain_one, grad_gain_query, grad_gain_key, grad_gain_two)
    normed1_low, sum_gate = lax.optimization_barrier((pair_sum(normed1_term, 0), sum_gate))
    d_normed1 = lax.psum_scatter(normed1_low, "outer", scatter_dimension=0, tiled=True)
    qkv_term = jnp.einsum("td,tc->dc", first_normed, d_qkv, preferred_element_type=jnp.float32)
    router_term = jnp.einsum("te,td->ed", d_logits, normed2, preferred_element_type=jnp.float32)
    router_term = expert_major(router_term).T
    gain_cols = -(-sum(term.shape[0] for term in gain_terms) // w_rows)
    flat_gains = jnp.concatenate(gain_terms)
    flat_gains = jnp.pad(flat_gains, (0, gain_cols * w_rows - flat_gains.shape[0]))
    gain_block = jnp.broadcast_to(
        flat_gains.reshape(w_rows, gain_cols)[None], (n_dp * n_expert, w_rows, gain_cols)
    ).reshape(model_dim, gain_cols)
    tail_cols = -(-(n_routed + gain_cols) // head_dim) * head_dim
    spare = jnp.zeros((model_dim, tail_cols - n_routed - gain_cols), jnp.float32)
    grad_blocks = (
        jnp.concatenate([qkv_term, router_term, gain_block, spare], axis=1)
        .astype(jnp.bfloat16)
        .reshape(n_expert, n_dp, w_rows, -1)
    )
    grad_blocks = lax.all_to_all(grad_blocks, "expert", split_axis=0, concat_axis=0, tiled=True)
    upper_low, d_normed1, grad_blocks = lax.optimization_barrier(
        (grad_upper, d_normed1, grad_blocks)
    )
    sum_upper = lax.psum_scatter(upper_low, "outer", scatter_dimension=1, tiled=True)
    d_tok_norm = norm1_pull(row_major(d_normed1).astype(jnp.float32))[0]
    grad_input = (d_resid + d_tok_norm)[None]
    sum_gate = sum_gate.astype(jnp.float32)
    sum_upper = sum_upper.astype(jnp.float32)
    sum_down = sum_down.astype(jnp.float32).transpose(0, 2, 1)
    grad_blocks = jnp.sum(grad_blocks.astype(jnp.float32), axis=0).astype(jnp.bfloat16)
    grad_blocks = lax.all_to_all(grad_blocks, DP, split_axis=0, concat_axis=0, tiled=True)
    out_term, grad_blocks = lax.optimization_barrier((out_term.astype(jnp.bfloat16), grad_blocks))
    out_term = lax.all_to_all(
        out_term.reshape((n_expert,) + w_out.shape),
        "expert",
        split_axis=0,
        concat_axis=0,
        tiled=True,
    )
    grad_blocks = grad_blocks.astype(jnp.float32)

    def gather_heads(first):
        picked = grad_blocks[:, :, first : first + head_dim]
        picked = jnp.sum(picked.reshape(heads_kv, share, w_rows, head_dim), axis=1)
        return picked.transpose(1, 0, 2).reshape(w_rows, heads_kv * head_dim)

    sum_wq = grad_blocks[:, :, :q_cols].transpose(1, 0, 2).reshape(w_rows, heads_q * head_dim)
    sum_wk = gather_heads(q_cols)
    sum_wv = gather_heads(q_cols + head_dim)
    tail_sum = jnp.sum(grad_blocks[:, :, qkv_cols:], axis=0)
    sum_wr = tail_sum[:, :n_routed]
    flat_gains = tail_sum[:, n_routed : n_routed + gain_cols].reshape(-1)
    ends = (model_dim, model_dim + head_dim, model_dim + 2 * head_dim, 2 * model_dim + 2 * head_dim)
    sum_one = flat_gains[: ends[0]]
    sum_query = flat_gains[ends[0] : ends[1]]
    sum_key = flat_gains[ends[1] : ends[2]]
    sum_two = flat_gains[ends[2] : ends[3]]
    sum_wo = jnp.sum(out_term.astype(jnp.float32), axis=0)
    return (
        output,
        grad_input,
        sum_one,
        sum_wq,
        sum_wk,
        sum_wv,
        sum_query,
        sum_key,
        sum_wo,
        sum_two,
        sum_wr,
        sum_gate,
        sum_upper,
        sum_down,
    )


def solution(mesh):
    n_dp, n_expert = mesh.devices.shape
    view = jax.sharding.Mesh(
        mesh.devices.reshape(n_dp // 2, 2, n_expert), ("outer", "core", "expert")
    )
    rows = P((*DP, "expert"), None)
    return jax.shard_map(
        shards,
        mesh=view,
        in_specs=(
            P("expert", DP, None),
            P(),
            rows,
            rows,
            rows,
            P(),
            P(),
            rows,
            P(),
            rows,
            P("expert", None, None),
            P("expert", None, None),
            P("expert", None, None),
            P("expert", DP),
            P("expert", DP, None),
            P("expert", DP, None),
        ),
        out_specs=(
            P("expert", DP, None),
            P("expert", DP, None),
            P(),
            rows,
            rows,
            rows,
            P(),
            P(),
            rows,
            P(),
            rows,
            P("expert", DP, None),
            P("expert", DP, None),
            P("expert", None, DP),
        ),
        check_vma=False,
    )
```

```python
import jax
import jax.numpy as jnp
from jax import lax
from jax.sharding import PartitionSpec as P

CAP = 48
DP = ("outer", "core")


EPSILON = 1e-06
THETA_BASE = 1000000.0
MASKED = -1e30


def norm_rows(values, gain):
    return values * lax.rsqrt(jnp.mean(values * values, axis=-1, keepdims=True) + EPSILON) * gain


def rotate_half(values):
    middle = values.shape[-1] // 2
    return jnp.concatenate([-values[..., middle:], values[..., :middle]], axis=-1)


def rope_tables(positions, head_width):
    freq_index = jnp.arange(head_width // 2).astype(jnp.float32)
    inverse = THETA_BASE ** (-2.0 * freq_index / head_width)
    angles = positions.astype(jnp.float32)[:, None] * inverse[None, :]
    angles = jnp.concatenate([angles, angles], axis=-1)
    return (jnp.cos(angles)[:, None, :], jnp.sin(angles)[:, None, :])


def prepare_heads(raw, gain, cosine_table, sine_table, heads):
    normed = norm_rows(raw.reshape(raw.shape[0], heads, -1), gain)
    return normed * cosine_table + rotate_half(normed) * sine_table


def silu_product(gate_pre, up_pre):
    return jax.nn.silu(gate_pre) * up_pre


def pair_sum(values, axis):
    values = values.astype(jnp.bfloat16)
    size = values.shape[axis] // lax.axis_size(DP)
    split = values.shape[:axis] + (-1, 2, size) + values.shape[axis + 1 :]
    merged = values.shape[:axis] + (-1,) + values.shape[axis + 1 :]
    core = lax.axis_index("core")

    def pick(index):
        return lax.dynamic_index_in_dim(values.reshape(split), index, axis + 1, keepdims=False)

    arrived = lax.ppermute(pick(1 - core), "core", [(0, 1), (1, 0)])
    total = pick(core).astype(jnp.float32) + arrived.astype(jnp.float32)
    return total.astype(jnp.bfloat16).reshape(merged)


def expert_term(rows, weights):
    return pair_sum(
        jnp.einsum("erd,erf->edf", rows, weights, preferred_element_type=jnp.float32), 1
    )


def slot_table(chosen, n_routed):
    rows, top_count = chosen.shape[-2:]
    flat = chosen.reshape(-1, rows * top_count)
    onehot = (flat[:, :, None] == jnp.arange(n_routed, dtype=jnp.int32)).astype(jnp.float32)
    index = jnp.arange(rows * top_count, dtype=jnp.int32)
    earlier = (index[:, None] > index[None, :]).astype(jnp.bfloat16)
    counts = jnp.einsum(
        "ij,sje->sie", earlier, onehot.astype(jnp.bfloat16), preferred_element_type=jnp.float32
    )
    ranks = jnp.sum(counts * onehot, axis=2).astype(jnp.int32)
    return (flat * CAP + ranks).reshape(chosen.shape)


def choose_gates(normed, router, chosen):
    logits = jnp.dot(normed, router, preferred_element_type=jnp.float32)
    experts = jnp.arange(router.shape[1], dtype=jnp.int32)
    onehot = (chosen[:, :, None] == experts).astype(jnp.float32)
    return (jax.nn.softmax(jnp.sum(onehot * logits[:, None, :], axis=2), axis=-1), onehot)


def shards(
    tokens,
    norm1,
    w_query,
    key_projection,
    value_projection,
    q_gain,
    key_norm_gain,
    w_out,
    norm2,
    w_router,
    w_gate,
    w_up,
    w_down,
    segments,
    routes,
    grad_out,
):
    tok_in = tokens[0].astype(jnp.float32)
    tok_rows, model_dim = tok_in.shape
    head_dim = q_gain.shape[0]
    heads_q = w_query.shape[1] // head_dim
    heads_kv = key_projection.shape[1] // head_dim
    n_dp = lax.axis_size(DP)
    n_expert = lax.axis_size("expert")
    w_rows = w_query.shape[0]
    own_heads = heads_q // n_dp
    share = n_dp // heads_kv
    q_cols = own_heads * head_dim
    n_routed = w_router.shape[1]
    top_count = routes.shape[2]
    score_scale = head_dim ** (-0.5)
    gain_one = norm1.astype(jnp.float32)
    gain_two = norm2.astype(jnp.float32)
    gain_query = q_gain.astype(jnp.float32)
    gain_key = key_norm_gain.astype(jnp.float32)
    normed1_f, norm1_pull = jax.vjp(norm_rows, tok_in, gain_one)
    segment = lax.all_gather(segments[0].astype(jnp.bfloat16), DP, axis=0, tiled=True)
    seq_rows = segment.shape[0]

    def heads_of(matrix):
        return matrix.reshape(w_rows, heads_kv, 1, 1, head_dim)

    pairs = jnp.concatenate([heads_of(key_projection), heads_of(value_projection)], axis=3)
    pairs = jnp.broadcast_to(pairs, (w_rows, heads_kv, share // 2, 2, head_dim))
    blocks = jnp.concatenate(
        [w_query.reshape(w_rows, n_dp, q_cols), pairs.reshape(w_rows, n_dp, head_dim)], axis=2
    ).transpose(1, 0, 2)
    core = lax.axis_index("core")
    swap = [(0, 1), (1, 0)]
    blocks = lax.all_to_all(blocks, DP, split_axis=0, concat_axis=0, tiled=True)

    def spread_expert(piece):
        copies = jnp.broadcast_to(piece[None], (n_expert,) + piece.shape)
        return lax.all_to_all(copies, "expert", split_axis=0, concat_axis=0, tiled=True)

    def expert_major(values):
        split = values.reshape(values.shape[0], n_dp, n_expert, w_rows)
        return split.transpose(0, 2, 1, 3).reshape(values.shape[0], model_dim)

    def row_major(values):
        split = values.reshape(values.shape[0], n_expert, n_dp, w_rows)
        return split.transpose(0, 2, 1, 3).reshape(values.shape[0], model_dim)

    first_normed = expert_major(normed1_f.astype(jnp.bfloat16))
    first_normed, blocks = lax.optimization_barrier((first_normed, blocks))
    first_normed = lax.all_gather(first_normed, DP, axis=0, tiled=True)
    all_routes = lax.all_gather(routes[0], "expert", axis=0)
    full_router = lax.all_gather(w_router, (*DP, "expert"), axis=0, tiled=True)
    blocks, w_out, all_routes, segment, full_router = lax.optimization_barrier(
        (spread_expert(blocks), w_out, all_routes, segment, full_router)
    )
    blocks = blocks.reshape(model_dim, -1)
    held_one = blocks[:, q_cols:]
    held_two = lax.ppermute(held_one, "core", swap)
    own_weights = jnp.concatenate(
        [
            blocks[:, :q_cols],
            jnp.where(core == 0, held_one, held_two),
            jnp.where(core == 0, held_two, held_one),
        ],
        axis=1,
    )
    own_out = spread_expert(w_out).reshape(q_cols, model_dim)
    raw = jnp.dot(first_normed, own_weights, preferred_element_type=jnp.float32)
    q_raw = raw[:, :q_cols]
    key_unrotated = raw[:, q_cols : q_cols + head_dim]
    value_low = raw[:, q_cols + head_dim :].astype(jnp.bfloat16)
    positions = jnp.arange(seq_rows, dtype=jnp.int32)
    cosine_table, sine_table = rope_tables(positions, head_dim)
    q_rot, query_pull = jax.vjp(
        lambda raw_in, gain_in: prepare_heads(raw_in, gain_in, cosine_table, sine_table, own_heads),
        q_raw,
        gain_query,
    )
    k_rot, key_pull = jax.vjp(
        lambda raw_in, gain_in: prepare_heads(raw_in, gain_in, cosine_table, sine_table, 1),
        key_unrotated,
        gain_key,
    )
    q_low = q_rot.astype(jnp.bfloat16)
    key_low = k_rot.astype(jnp.bfloat16).reshape(seq_rows, head_dim)
    allowed = (
        (positions[:, None] >= positions[None, :]) & (segment[:, None] == segment[None, :])
    )[None]

    def raw_weights():
        score = jnp.einsum("tgd,sd->gts", q_low, key_low, preferred_element_type=jnp.float32)
        return jnp.where(allowed, jnp.exp(score * score_scale), 0.0)

    weights = raw_weights()
    inverse_sum = 1.0 / jnp.sum(weights, axis=-1)
    attn_heads = (
        jnp.einsum(
            "gts,sd->gtd", weights.astype(jnp.bfloat16), value_low, preferred_element_type=jnp.float32
        )
        * inverse_sum[..., None]
    )
    attn_low = attn_heads.transpose(1, 0, 2).reshape(seq_rows, q_cols).astype(jnp.bfloat16)
    branch_term = jnp.dot(attn_low, own_out, preferred_element_type=jnp.float32)
    branch_low, late_grad = lax.optimization_barrier((branch_term.astype(jnp.bfloat16), grad_out[0]))
    branch = lax.psum_scatter(branch_low, DP, scatter_dimension=0, tiled=True)
    branch, all_grad = lax.optimization_barrier((branch, spread_expert(late_grad)))
    residual = tok_in + branch.astype(jnp.float32)
    normed2_f, norm2_pull = jax.vjp(norm_rows, residual, gain_two)
    normed2 = normed2_f.astype(jnp.bfloat16)
    all_normed = spread_expert(normed2)
    chosen = routes[0]
    gate_probs, onehot = choose_gates(normed2, full_router, chosen)
    slot_count = n_routed * CAP
    slots = slot_table(chosen, n_routed)
    slot_hits = slots[:, :, None] == jnp.arange(slot_count, dtype=jnp.int32)
    route_picks = slot_hits.astype(jnp.bfloat16).transpose(1, 0, 2)
    token_picks = jnp.any(slot_hits, axis=1).astype(jnp.bfloat16)
    held = w_gate.shape[0]
    first_slot = lax.axis_index("expert") * (held * CAP)
    all_hits = (slot_table(all_routes, n_routed) - first_slot)[..., None] == jnp.arange(
        held * CAP, dtype=jnp.int32
    )
    all_picks = jnp.any(all_hits, axis=2).astype(jnp.bfloat16)

    def to_slots(rows):
        return jnp.einsum("stl,std->sld", all_picks, rows, preferred_element_type=jnp.float32)

    def by_expert(rows):
        rows = rows.reshape(n_expert, held, CAP, model_dim).transpose(1, 0, 2, 3)
        return rows.reshape(held, n_expert * CAP, model_dim)

    all_gates, _ = choose_gates(
        all_normed.reshape(-1, model_dim), full_router, all_routes.reshape(-1, top_count)
    )
    all_gates = all_gates.reshape(all_routes.shape)
    slot_gate = jnp.sum(jnp.where(all_hits, all_gates[..., None], 0.0), axis=(1, 2))
    received = by_expert(to_slots(all_normed).astype(jnp.bfloat16))
    d_recv = by_expert((slot_gate[:, :, None] * to_slots(all_grad)).astype(jnp.bfloat16))
    gate_pre = jnp.einsum("erd,edf->erf", received, w_gate, preferred_element_type=jnp.float32)
    up_pre = jnp.einsum("erd,edf->erf", received, w_up, preferred_element_type=jnp.float32)
    hidden_f, act_pull = jax.vjp(silu_product, gate_pre, up_pre)
    hidden = hidden_f.astype(jnp.bfloat16)
    expert_out = jnp.einsum(
        "erf,efd->erd", hidden, w_down, preferred_element_type=jnp.float32
    ).astype(jnp.bfloat16)
    returned = lax.all_to_all(
        expert_out, "expert", split_axis=1, concat_axis=0, tiled=True
    ).reshape(n_routed * CAP, model_dim)
    route_out = jnp.einsum(
        "kts,sd->ktd", route_picks, returned, preferred_element_type=jnp.float32
    )
    mixture = jnp.sum(gate_probs.T[:, :, None] * route_out, axis=0)
    output = (residual + mixture).astype(jnp.bfloat16)[None]
    grad_rows = grad_out[0].astype(jnp.float32)
    d_gates = jnp.sum(grad_rows[None] * route_out, axis=-1).T
    d_picked = gate_probs * (d_gates - jnp.sum(gate_probs * d_gates, axis=1, keepdims=True))
    d_logits = jnp.sum(onehot * d_picked[:, :, None], axis=1).astype(jnp.bfloat16)
    d_hidden = jnp.einsum("erd,efd->erf", d_recv, w_down, preferred_element_type=jnp.float32)
    grad_down = jnp.einsum(
        "erd,erf->edf", d_recv, hidden, preferred_element_type=jnp.float32
    ).astype(jnp.bfloat16)
    d_gate_f, d_up_f = act_pull(d_hidden)
    d_gate = d_gate_f.astype(jnp.bfloat16)
    d_up = d_up_f.astype(jnp.bfloat16)
    grad_gate = expert_term(received, d_gate)
    grad_upper = expert_term(received, d_up)
    d_in = (
        jnp.einsum("erf,edf->erd", d_gate, w_gate, preferred_element_type=jnp.float32)
        + jnp.einsum("erf,edf->erd", d_up, w_up, preferred_element_type=jnp.float32)
    ).astype(jnp.bfloat16)
    d_back = lax.all_to_all(d_in, "expert", split_axis=1, concat_axis=0, tiled=True).reshape(
        n_routed * CAP, model_dim
    )
    d_normed2 = jnp.dot(token_picks, d_back, preferred_element_type=jnp.float32)
    d_normed2 = d_normed2 + jnp.einsum(
        "te,de->td", d_logits, full_router, preferred_element_type=jnp.float32
    )
    d_resid_norm, grad_gain_two = norm2_pull(d_normed2)
    d_resid = grad_rows + d_resid_norm
    sum_down = lax.psum_scatter(grad_down, DP, scatter_dimension=1, tiled=True)
    d_branch, sum_down = lax.optimization_barrier((d_resid.astype(jnp.bfloat16), sum_down))
    all_branch = lax.all_gather(d_branch, DP, axis=0, tiled=True)
    gate_low, upper_low, all_branch = lax.optimization_barrier((grad_gate, grad_upper, all_branch))
    sum_gate = lax.psum_scatter(gate_low, "outer", scatter_dimension=1, tiled=True)
    sum_upper = lax.psum_scatter(upper_low, "outer", scatter_dimension=1, tiled=True)
    d_attn = jnp.einsum(
        "td,cd->tc", all_branch, own_out, preferred_element_type=jnp.float32
    ).astype(jnp.bfloat16)
    d_attn_heads = d_attn.reshape(seq_rows, own_heads, head_dim)
    delta = jnp.sum(d_attn_heads.transpose(1, 0, 2).astype(jnp.float32) * attn_heads, axis=-1)
    probs = raw_weights() * inverse_sum[..., None]
    d_probs = jnp.einsum(
        "tgd,sd->gts", d_attn_heads, value_low, preferred_element_type=jnp.float32
    )
    d_score = (probs * (d_probs - delta[..., None])).astype(jnp.bfloat16)
    d_query = score_scale * jnp.einsum(
        "gts,sd->tgd", d_score, key_low, preferred_element_type=jnp.float32
    )
    d_keys = score_scale * jnp.einsum(
        "gts,tgd->sd", d_score, q_low, preferred_element_type=jnp.float32
    )
    d_values = jnp.einsum(
        "gts,tgd->sd", probs.astype(jnp.bfloat16), d_attn_heads, preferred_element_type=jnp.float32
    )
    d_q_f, grad_gain_query = query_pull(d_query)
    d_k_f, grad_gain_key = key_pull(d_keys[:, None, :])
    d_qkv = jnp.concatenate([d_q_f, d_k_f, d_values], axis=1).astype(jnp.bfloat16)
    out_term = jnp.einsum("tc,td->cd", attn_low, all_branch, preferred_element_type=jnp.float32)
    normed1_term = jnp.einsum("tc,dc->td", d_qkv, own_weights, preferred_element_type=jnp.float32)
    grad_gain_one = (
        row_major(jnp.sum(normed1_term * first_normed.astype(jnp.float32), axis=0)[None])[0]
        / gain_one
    )
    gain_terms = (grad_gain_one, grad_gain_query, grad_gain_key, grad_gain_two)
    normed1_pair = pair_sum(normed1_term, 0)
    qkv_term = jnp.einsum("td,tc->dc", first_normed, d_qkv, preferred_element_type=jnp.float32)
    key_term = qkv_term[:, q_cols : q_cols + head_dim]
    value_term = qkv_term[:, q_cols + head_dim :]
    sent = jnp.where(core == 0, value_term, key_term).astype(jnp.bfloat16)
    arrived = lax.ppermute(sent, "core", swap).astype(jnp.float32)
    held_term = jnp.where(core == 0, key_term, value_term) + arrived
    router_term = jnp.einsum("te,td->ed", d_logits, normed2, preferred_element_type=jnp.float32)
    router_term = expert_major(router_term).T
    gain_cols = -(-sum(term.shape[0] for term in gain_terms) // w_rows)
    flat_gains = jnp.concatenate(gain_terms)
    flat_gains = jnp.pad(flat_gains, (0, gain_cols * w_rows - flat_gains.shape[0]))
    gain_block = jnp.broadcast_to(
        flat_gains.reshape(w_rows, gain_cols)[None], (n_dp * n_expert, w_rows, gain_cols)
    ).reshape(model_dim, gain_cols)
    tail_cols = -(-(n_routed + gain_cols) // head_dim) * head_dim
    spare = jnp.zeros((model_dim, tail_cols - n_routed - gain_cols), jnp.float32)
    grad_blocks = (
        jnp.concatenate([qkv_term[:, :q_cols], held_term, router_term, gain_block, spare], axis=1)
        .astype(jnp.bfloat16)
        .reshape(n_expert, n_dp, w_rows, -1)
    )
    grad_blocks = lax.all_to_all(grad_blocks, "expert", split_axis=0, concat_axis=0, tiled=True)
    sum_gate = sum_gate.astype(jnp.float32)
    sum_upper = sum_upper.astype(jnp.float32)
    sum_down = sum_down.astype(jnp.float32).transpose(0, 2, 1)
    grad_blocks = jnp.sum(grad_blocks.astype(jnp.float32), axis=0).astype(jnp.bfloat16)
    grad_blocks = lax.all_to_all(grad_blocks, DP, split_axis=0, concat_axis=0, tiled=True)
    normed1_low, sum_gate, sum_upper, grad_blocks = lax.optimization_barrier(
        (normed1_pair, sum_gate, sum_upper, grad_blocks)
    )
    d_normed1 = lax.psum_scatter(normed1_low, "outer", scatter_dimension=0, tiled=True)
    d_tok_norm = norm1_pull(row_major(d_normed1).astype(jnp.float32))[0]
    grad_input = (d_resid + d_tok_norm)[None]
    out_term, grad_blocks = lax.optimization_barrier((out_term.astype(jnp.bfloat16), grad_blocks))
    out_term = lax.all_to_all(
        out_term.reshape((n_expert,) + w_out.shape),
        "expert",
        split_axis=0,
        concat_axis=0,
        tiled=True,
    )
    grad_blocks = grad_blocks.astype(jnp.float32)

    def gather_heads(which):
        picked = grad_blocks[:, :, q_cols : q_cols + head_dim]
        picked = picked.reshape(heads_kv, share // 2, 2, w_rows, head_dim)[:, :, which]
        return jnp.sum(picked, axis=1).transpose(1, 0, 2).reshape(w_rows, heads_kv * head_dim)

    sum_wq = grad_blocks[:, :, :q_cols].transpose(1, 0, 2).reshape(w_rows, heads_q * head_dim)
    sum_wk = gather_heads(0)
    sum_wv = gather_heads(1)
    tail_sum = jnp.sum(grad_blocks[:, :, q_cols + head_dim :], axis=0)
    sum_wr = tail_sum[:, :n_routed]
    flat_gains = tail_sum[:, n_routed : n_routed + gain_cols].reshape(-1)
    ends = (model_dim, model_dim + head_dim, model_dim + 2 * head_dim, 2 * model_dim + 2 * head_dim)
    sum_one = flat_gains[: ends[0]]
    sum_query = flat_gains[ends[0] : ends[1]]
    sum_key = flat_gains[ends[1] : ends[2]]
    sum_two = flat_gains[ends[2] : ends[3]]
    sum_wo = jnp.sum(out_term.astype(jnp.float32), axis=0)
    return (
        output,
        grad_input,
        sum_one,
        sum_wq,
        sum_wk,
        sum_wv,
        sum_query,
        sum_key,
        sum_wo,
        sum_two,
        sum_wr,
        sum_gate,
        sum_upper,
        sum_down,
    )


def solution(mesh):
    n_dp, n_expert = mesh.devices.shape
    view = jax.sharding.Mesh(
        mesh.devices.reshape(n_dp // 2, 2, n_expert), ("outer", "core", "expert")
    )
    rows = P((*DP, "expert"), None)
    return jax.shard_map(
        shards,
        mesh=view,
        in_specs=(
            P("expert", DP, None),
            P(),
            rows,
            rows,
            rows,
            P(),
            P(),
            rows,
            P(),
            rows,
            P("expert", None, None),
            P("expert", None, None),
            P("expert", None, None),
            P("expert", DP),
            P("expert", DP, None),
            P("expert", DP, None),
        ),
        out_specs=(
            P("expert", DP, None),
            P("expert", DP, None),
            P(),
            rows,
            rows,
            rows,
            P(),
            P(),
            rows,
            P(),
            rows,
            P("expert", DP, None),
            P("expert", DP, None),
            P("expert", None, DP),
        ),
        check_vma=False,
    )
```

```python
import jax
import jax.numpy as jnp
from jax import lax
from jax.sharding import PartitionSpec as P

CAP = 48
DP = ("outer", "core")


EPSILON = 1e-06
THETA_BASE = 1000000.0
MASKED = -1e30


def norm_rows(values, gain):
    return values * lax.rsqrt(jnp.mean(values * values, axis=-1, keepdims=True) + EPSILON) * gain


def rotate_half(values):
    middle = values.shape[-1] // 2
    return jnp.concatenate([-values[..., middle:], values[..., :middle]], axis=-1)


def rope_tables(positions, head_width):
    freq_index = jnp.arange(head_width // 2).astype(jnp.float32)
    inverse = THETA_BASE ** (-2.0 * freq_index / head_width)
    angles = positions.astype(jnp.float32)[:, None] * inverse[None, :]
    angles = jnp.concatenate([angles, angles], axis=-1)
    return (jnp.cos(angles)[:, None, :], jnp.sin(angles)[:, None, :])


def prepare_heads(raw, gain, cosine_table, sine_table, heads):
    normed = norm_rows(raw.reshape(raw.shape[0], heads, -1), gain)
    return normed * cosine_table + rotate_half(normed) * sine_table


def silu_product(gate_pre, up_pre):
    return jax.nn.silu(gate_pre) * up_pre


def pair_sum(values, axis):
    values = values.astype(jnp.bfloat16)
    size = values.shape[axis] // lax.axis_size(DP)
    split = values.shape[:axis] + (-1, 2, size) + values.shape[axis + 1 :]
    merged = values.shape[:axis] + (-1,) + values.shape[axis + 1 :]
    core = lax.axis_index("core")

    def pick(index):
        return lax.dynamic_index_in_dim(values.reshape(split), index, axis + 1, keepdims=False)

    arrived = lax.ppermute(pick(1 - core), "core", [(0, 1), (1, 0)])
    total = pick(core).astype(jnp.float32) + arrived.astype(jnp.float32)
    return total.astype(jnp.bfloat16).reshape(merged)


def expert_term(rows, weights):
    return pair_sum(
        jnp.einsum("erd,erf->edf", rows, weights, preferred_element_type=jnp.float32), 1
    )


def slot_table(chosen, n_routed):
    rows, top_count = chosen.shape[-2:]
    flat = chosen.reshape(-1, rows * top_count)
    onehot = (flat[:, :, None] == jnp.arange(n_routed, dtype=jnp.int32)).astype(jnp.float32)
    index = jnp.arange(rows * top_count, dtype=jnp.int32)
    earlier = (index[:, None] > index[None, :]).astype(jnp.bfloat16)
    counts = jnp.einsum(
        "ij,sje->sie", earlier, onehot.astype(jnp.bfloat16), preferred_element_type=jnp.float32
    )
    ranks = jnp.sum(counts * onehot, axis=2).astype(jnp.int32)
    return (flat * CAP + ranks).reshape(chosen.shape)


def choose_gates(normed, router, chosen):
    logits = jnp.dot(normed, router, preferred_element_type=jnp.float32)
    experts = jnp.arange(router.shape[1], dtype=jnp.int32)
    onehot = (chosen[:, :, None] == experts).astype(jnp.float32)
    return (jax.nn.softmax(jnp.sum(onehot * logits[:, None, :], axis=2), axis=-1), onehot)


def shards(
    tokens,
    norm1,
    w_query,
    key_projection,
    value_projection,
    q_gain,
    key_norm_gain,
    w_out,
    norm2,
    w_router,
    w_gate,
    w_up,
    w_down,
    segments,
    routes,
    grad_out,
):
    tok_in = tokens[0].astype(jnp.float32)
    tok_rows, model_dim = tok_in.shape
    head_dim = q_gain.shape[0]
    heads_q = w_query.shape[1] // head_dim
    heads_kv = key_projection.shape[1] // head_dim
    n_dp = lax.axis_size(DP)
    n_expert = lax.axis_size("expert")
    w_rows = w_query.shape[0]
    own_heads = heads_q // n_dp
    share = n_dp // heads_kv
    q_cols = own_heads * head_dim
    n_routed = w_router.shape[1]
    top_count = routes.shape[2]
    score_scale = head_dim ** (-0.5)
    gain_one = norm1.astype(jnp.float32)
    gain_two = norm2.astype(jnp.float32)
    gain_query = q_gain.astype(jnp.float32)
    gain_key = key_norm_gain.astype(jnp.float32)
    normed1_f, norm1_pull = jax.vjp(norm_rows, tok_in, gain_one)
    segment = lax.all_gather(segments[0].astype(jnp.bfloat16), DP, axis=0, tiled=True)
    seq_rows = segment.shape[0]

    def heads_of(matrix):
        return matrix.reshape(w_rows, heads_kv, 1, 1, head_dim)

    pairs = jnp.concatenate([heads_of(key_projection), heads_of(value_projection)], axis=3)
    pairs = jnp.broadcast_to(pairs, (w_rows, heads_kv, share // 2, 2, head_dim))
    router_pad = jnp.pad(w_router, ((0, 0), (0, head_dim - n_routed)))
    blocks = jnp.concatenate(
        [
            w_query.reshape(w_rows, n_dp, q_cols),
            pairs.reshape(w_rows, n_dp, head_dim),
            jnp.broadcast_to(router_pad[:, None, :], (w_rows, n_dp, head_dim)),
        ],
        axis=2,
    ).transpose(1, 0, 2)
    core = lax.axis_index("core")
    swap = [(0, 1), (1, 0)]
    blocks = lax.all_to_all(blocks, DP, split_axis=0, concat_axis=0, tiled=True)

    def spread_expert(piece):
        copies = jnp.broadcast_to(piece[None], (n_expert,) + piece.shape)
        return lax.all_to_all(copies, "expert", split_axis=0, concat_axis=0, tiled=True)

    def expert_major(values):
        split = values.reshape(values.shape[0], n_dp, n_expert, w_rows)
        return split.transpose(0, 2, 1, 3).reshape(values.shape[0], model_dim)

    def row_major(values):
        split = values.reshape(values.shape[0], n_expert, n_dp, w_rows)
        return split.transpose(0, 2, 1, 3).reshape(values.shape[0], model_dim)

    first_normed = expert_major(normed1_f.astype(jnp.bfloat16))
    first_normed, blocks = lax.optimization_barrier((first_normed, blocks))
    first_normed = lax.all_gather(first_normed, DP, axis=0, tiled=True)
    all_routes = lax.all_gather(routes[0], "expert", axis=0)
    blocks, w_out, all_routes, segment = lax.optimization_barrier(
        (spread_expert(blocks), w_out, all_routes, segment)
    )
    blocks = blocks.reshape(model_dim, -1)
    kv_cols = q_cols + head_dim
    full_router = row_major(blocks[:, kv_cols : kv_cols + n_routed].T).T
    held_one = blocks[:, q_cols:kv_cols]
    held_two = lax.ppermute(held_one, "core", swap)
    own_weights = jnp.concatenate(
        [
            blocks[:, :q_cols],
            jnp.where(core == 0, held_one, held_two),
            jnp.where(core == 0, held_two, held_one),
        ],
        axis=1,
    )
    own_out = spread_expert(w_out).reshape(q_cols, model_dim)
    raw = jnp.dot(first_normed, own_weights, preferred_element_type=jnp.float32)
    q_raw = raw[:, :q_cols]
    key_unrotated = raw[:, q_cols : q_cols + head_dim]
    value_low = raw[:, q_cols + head_dim :].astype(jnp.bfloat16)
    positions = jnp.arange(seq_rows, dtype=jnp.int32)
    cosine_table, sine_table = rope_tables(positions, head_dim)
    q_rot, query_pull = jax.vjp(
        lambda raw_in, gain_in: prepare_heads(raw_in, gain_in, cosine_table, sine_table, own_heads),
        q_raw,
        gain_query,
    )
    k_rot, key_pull = jax.vjp(
        lambda raw_in, gain_in: prepare_heads(raw_in, gain_in, cosine_table, sine_table, 1),
        key_unrotated,
        gain_key,
    )
    q_low = q_rot.astype(jnp.bfloat16)
    key_low = k_rot.astype(jnp.bfloat16).reshape(seq_rows, head_dim)
    allowed = (
        (positions[:, None] >= positions[None, :]) & (segment[:, None] == segment[None, :])
    )[None]

    def raw_weights():
        score = jnp.einsum("tgd,sd->gts", q_low, key_low, preferred_element_type=jnp.float32)
        return jnp.where(allowed, jnp.exp(score * score_scale), 0.0)

    weights = raw_weights()
    inverse_sum = 1.0 / jnp.sum(weights, axis=-1)
    attn_heads = (
        jnp.einsum(
            "gts,sd->gtd", weights.astype(jnp.bfloat16), value_low, preferred_element_type=jnp.float32
        )
        * inverse_sum[..., None]
    )
    attn_low = attn_heads.transpose(1, 0, 2).reshape(seq_rows, q_cols).astype(jnp.bfloat16)
    branch_term = jnp.dot(attn_low, own_out, preferred_element_type=jnp.float32)
    branch_low, late_grad = lax.optimization_barrier((branch_term.astype(jnp.bfloat16), grad_out[0]))
    branch = lax.psum_scatter(branch_low, DP, scatter_dimension=0, tiled=True)
    branch, all_grad = lax.optimization_barrier((branch, spread_expert(late_grad)))
    residual = tok_in + branch.astype(jnp.float32)
    normed2_f, norm2_pull = jax.vjp(norm_rows, residual, gain_two)
    normed2 = normed2_f.astype(jnp.bfloat16)
    all_normed = spread_expert(normed2)
    chosen = routes[0]
    gate_probs, onehot = choose_gates(normed2, full_router, chosen)
    slot_count = n_routed * CAP
    slots = slot_table(chosen, n_routed)
    slot_hits = slots[:, :, None] == jnp.arange(slot_count, dtype=jnp.int32)
    route_picks = slot_hits.astype(jnp.bfloat16).transpose(1, 0, 2)
    token_picks = jnp.any(slot_hits, axis=1).astype(jnp.bfloat16)
    held = w_gate.shape[0]
    first_slot = lax.axis_index("expert") * (held * CAP)
    all_hits = (slot_table(all_routes, n_routed) - first_slot)[..., None] == jnp.arange(
        held * CAP, dtype=jnp.int32
    )
    all_picks = jnp.any(all_hits, axis=2).astype(jnp.bfloat16)

    def to_slots(rows):
        return jnp.einsum("stl,std->sld", all_picks, rows, preferred_element_type=jnp.float32)

    def by_expert(rows):
        rows = rows.reshape(n_expert, held, CAP, model_dim).transpose(1, 0, 2, 3)
        return rows.reshape(held, n_expert * CAP, model_dim)

    all_gates, _ = choose_gates(
        all_normed.reshape(-1, model_dim), full_router, all_routes.reshape(-1, top_count)
    )
    all_gates = all_gates.reshape(all_routes.shape)
    slot_gate = jnp.sum(jnp.where(all_hits, all_gates[..., None], 0.0), axis=(1, 2))
    received = by_expert(to_slots(all_normed).astype(jnp.bfloat16))
    d_recv = by_expert((slot_gate[:, :, None] * to_slots(all_grad)).astype(jnp.bfloat16))
    gate_pre = jnp.einsum("erd,edf->erf", received, w_gate, preferred_element_type=jnp.float32)
    up_pre = jnp.einsum("erd,edf->erf", received, w_up, preferred_element_type=jnp.float32)
    hidden_f, act_pull = jax.vjp(silu_product, gate_pre, up_pre)
    hidden = hidden_f.astype(jnp.bfloat16)
    expert_out = jnp.einsum(
        "erf,efd->erd", hidden, w_down, preferred_element_type=jnp.float32
    ).astype(jnp.bfloat16)
    returned = lax.all_to_all(
        expert_out, "expert", split_axis=1, concat_axis=0, tiled=True
    ).reshape(n_routed * CAP, model_dim)
    route_out = jnp.einsum(
        "kts,sd->ktd", route_picks, returned, preferred_element_type=jnp.float32
    )
    mixture = jnp.sum(gate_probs.T[:, :, None] * route_out, axis=0)
    output = (residual + mixture).astype(jnp.bfloat16)[None]
    grad_rows = grad_out[0].astype(jnp.float32)
    d_gates = jnp.sum(grad_rows[None] * route_out, axis=-1).T
    d_picked = gate_probs * (d_gates - jnp.sum(gate_probs * d_gates, axis=1, keepdims=True))
    d_logits = jnp.sum(onehot * d_picked[:, :, None], axis=1).astype(jnp.bfloat16)
    d_hidden = jnp.einsum("erd,efd->erf", d_recv, w_down, preferred_element_type=jnp.float32)
    grad_down = jnp.einsum(
        "erd,erf->edf", d_recv, hidden, preferred_element_type=jnp.float32
    ).astype(jnp.bfloat16)
    d_gate_f, d_up_f = act_pull(d_hidden)
    d_gate = d_gate_f.astype(jnp.bfloat16)
    d_up = d_up_f.astype(jnp.bfloat16)
    grad_gate = expert_term(received, d_gate)
    grad_upper = expert_term(received, d_up)
    d_in = (
        jnp.einsum("erf,edf->erd", d_gate, w_gate, preferred_element_type=jnp.float32)
        + jnp.einsum("erf,edf->erd", d_up, w_up, preferred_element_type=jnp.float32)
    ).astype(jnp.bfloat16)
    d_back = lax.all_to_all(d_in, "expert", split_axis=1, concat_axis=0, tiled=True).reshape(
        n_routed * CAP, model_dim
    )
    d_normed2 = jnp.dot(token_picks, d_back, preferred_element_type=jnp.float32)
    d_normed2 = d_normed2 + jnp.einsum(
        "te,de->td", d_logits, full_router, preferred_element_type=jnp.float32
    )
    d_resid_norm, grad_gain_two = norm2_pull(d_normed2)
    d_resid = grad_rows + d_resid_norm
    sum_down = lax.psum_scatter(grad_down, DP, scatter_dimension=1, tiled=True)
    d_branch, sum_down = lax.optimization_barrier((d_resid.astype(jnp.bfloat16), sum_down))
    all_branch = lax.all_gather(d_branch, DP, axis=0, tiled=True)
    gate_low, upper_low, all_branch = lax.optimization_barrier((grad_gate, grad_upper, all_branch))
    sum_gate = lax.psum_scatter(gate_low, "outer", scatter_dimension=1, tiled=True)
    sum_upper = lax.psum_scatter(upper_low, "outer", scatter_dimension=1, tiled=True)
    d_attn = jnp.einsum(
        "td,cd->tc", all_branch, own_out, preferred_element_type=jnp.float32
    ).astype(jnp.bfloat16)
    d_attn_heads = d_attn.reshape(seq_rows, own_heads, head_dim)
    delta = jnp.sum(d_attn_heads.transpose(1, 0, 2).astype(jnp.float32) * attn_heads, axis=-1)
    probs = raw_weights() * inverse_sum[..., None]
    d_probs = jnp.einsum(
        "tgd,sd->gts", d_attn_heads, value_low, preferred_element_type=jnp.float32
    )
    d_score = (probs * (d_probs - delta[..., None])).astype(jnp.bfloat16)
    d_query = score_scale * jnp.einsum(
        "gts,sd->tgd", d_score, key_low, preferred_element_type=jnp.float32
    )
    d_keys = score_scale * jnp.einsum(
        "gts,tgd->sd", d_score, q_low, preferred_element_type=jnp.float32
    )
    d_values = jnp.einsum(
        "gts,tgd->sd", probs.astype(jnp.bfloat16), d_attn_heads, preferred_element_type=jnp.float32
    )
    d_q_f, grad_gain_query = query_pull(d_query)
    d_k_f, grad_gain_key = key_pull(d_keys[:, None, :])
    d_qkv = jnp.concatenate([d_q_f, d_k_f, d_values], axis=1).astype(jnp.bfloat16)
    out_term = jnp.einsum("tc,td->cd", attn_low, all_branch, preferred_element_type=jnp.float32)
    normed1_term = jnp.einsum("tc,dc->td", d_qkv, own_weights, preferred_element_type=jnp.float32)
    grad_gain_one = (
        row_major(jnp.sum(normed1_term * first_normed.astype(jnp.float32), axis=0)[None])[0]
        / gain_one
    )
    gain_terms = (grad_gain_one, grad_gain_query, grad_gain_key, grad_gain_two)
    normed1_pair = pair_sum(normed1_term, 0)
    qkv_term = jnp.einsum("td,tc->dc", first_normed, d_qkv, preferred_element_type=jnp.float32)
    key_term = qkv_term[:, q_cols : q_cols + head_dim]
    value_term = qkv_term[:, q_cols + head_dim :]
    sent = jnp.where(core == 0, value_term, key_term).astype(jnp.bfloat16)
    arrived = lax.ppermute(sent, "core", swap).astype(jnp.float32)
    held_term = jnp.where(core == 0, key_term, value_term) + arrived
    router_term = jnp.einsum("te,td->ed", d_logits, normed2, preferred_element_type=jnp.float32)
    router_term = expert_major(router_term).T
    gain_cols = -(-sum(term.shape[0] for term in gain_terms) // w_rows)
    flat_gains = jnp.concatenate(gain_terms)
    flat_gains = jnp.pad(flat_gains, (0, gain_cols * w_rows - flat_gains.shape[0]))
    gain_block = jnp.broadcast_to(
        flat_gains.reshape(w_rows, gain_cols)[None], (n_dp * n_expert, w_rows, gain_cols)
    ).reshape(model_dim, gain_cols)
    tail_cols = -(-(n_routed + gain_cols) // head_dim) * head_dim
    spare = jnp.zeros((model_dim, tail_cols - n_routed - gain_cols), jnp.float32)
    grad_blocks = (
        jnp.concatenate([qkv_term[:, :q_cols], held_term, router_term, gain_block, spare], axis=1)
        .astype(jnp.bfloat16)
        .reshape(n_expert, n_dp, w_rows, -1)
    )
    grad_blocks = lax.all_to_all(grad_blocks, "expert", split_axis=0, concat_axis=0, tiled=True)
    sum_gate = sum_gate.astype(jnp.float32)
    sum_upper = sum_upper.astype(jnp.float32)
    sum_down = sum_down.astype(jnp.float32).transpose(0, 2, 1)
    grad_blocks = jnp.sum(grad_blocks.astype(jnp.float32), axis=0).astype(jnp.bfloat16)
    grad_blocks = lax.all_to_all(grad_blocks, DP, split_axis=0, concat_axis=0, tiled=True)
    normed1_low, sum_gate, sum_upper, grad_blocks = lax.optimization_barrier(
        (normed1_pair, sum_gate, sum_upper, grad_blocks)
    )
    d_normed1 = lax.psum_scatter(normed1_low, "outer", scatter_dimension=0, tiled=True)
    d_tok_norm = norm1_pull(row_major(d_normed1).astype(jnp.float32))[0]
    grad_input = (d_resid + d_tok_norm)[None]
    out_term, grad_blocks = lax.optimization_barrier((out_term.astype(jnp.bfloat16), grad_blocks))
    out_term = lax.all_to_all(
        out_term.reshape((n_expert,) + w_out.shape),
        "expert",
        split_axis=0,
        concat_axis=0,
        tiled=True,
    )
    grad_blocks = grad_blocks.astype(jnp.float32)

    def gather_heads(which):
        picked = grad_blocks[:, :, q_cols : q_cols + head_dim]
        picked = picked.reshape(heads_kv, share // 2, 2, w_rows, head_dim)[:, :, which]
        return jnp.sum(picked, axis=1).transpose(1, 0, 2).reshape(w_rows, heads_kv * head_dim)

    sum_wq = grad_blocks[:, :, :q_cols].transpose(1, 0, 2).reshape(w_rows, heads_q * head_dim)
    sum_wk = gather_heads(0)
    sum_wv = gather_heads(1)
    tail_sum = jnp.sum(grad_blocks[:, :, q_cols + head_dim :], axis=0)
    sum_wr = tail_sum[:, :n_routed]
    flat_gains = tail_sum[:, n_routed : n_routed + gain_cols].reshape(-1)
    ends = (model_dim, model_dim + head_dim, model_dim + 2 * head_dim, 2 * model_dim + 2 * head_dim)
    sum_one = flat_gains[: ends[0]]
    sum_query = flat_gains[ends[0] : ends[1]]
    sum_key = flat_gains[ends[1] : ends[2]]
    sum_two = flat_gains[ends[2] : ends[3]]
    sum_wo = jnp.sum(out_term.astype(jnp.float32), axis=0)
    return (
        output,
        grad_input,
        sum_one,
        sum_wq,
        sum_wk,
        sum_wv,
        sum_query,
        sum_key,
        sum_wo,
        sum_two,
        sum_wr,
        sum_gate,
        sum_upper,
        sum_down,
    )


def solution(mesh):
    n_dp, n_expert = mesh.devices.shape
    view = jax.sharding.Mesh(
        mesh.devices.reshape(n_dp // 2, 2, n_expert), ("outer", "core", "expert")
    )
    rows = P((*DP, "expert"), None)
    return jax.shard_map(
        shards,
        mesh=view,
        in_specs=(
            P("expert", DP, None),
            P(),
            rows,
            rows,
            rows,
            P(),
            P(),
            rows,
            P(),
            rows,
            P("expert", None, None),
            P("expert", None, None),
            P("expert", None, None),
            P("expert", DP),
            P("expert", DP, None),
            P("expert", DP, None),
        ),
        out_specs=(
            P("expert", DP, None),
            P("expert", DP, None),
            P(),
            rows,
            rows,
            rows,
            P(),
            P(),
            rows,
            P(),
            rows,
            P("expert", DP, None),
            P("expert", DP, None),
            P("expert", None, DP),
        ),
        check_vma=False,
    )
```
